256 devices in a mesh: tm: 32 (over x_lo, z, core), space: 8 (over x_hi, y).
Axes of the slice: x: 4 (x_hi: 2, x_lo: 2; x = x_hi * 2 + x_lo), y: 4, z: 8, core: 2. Of those that a mesh axis runs over, the one named last changes fastest.
Arguments:
- start_disp: float32 [32, 3, 4, 256, 256], P('tm', None, None, 'space'), may hold values from -0.2 to 0.2
- start_vel: float32 [32, 3, 4, 256, 256], P('tm', None, None, 'space'), may hold values from -0.2 to 0.2
- start_visc: float32 [32, 3, 4, 256, 256], P('tm', None, None, 'space'), may hold values from -0.2 to 0.2
- init_state: float32 [3, 3, 4, 256, 256], P(None, None, None, 'space'), may hold values from -0.2 to 0.2
- inv_mass: float32 [4, 256, 256], P(None, 'space'), may hold values from 0.35 to 1
- damping_rate: float32 [4, 256, 256], P(None, 'space'), may hold values from 0.002 to 0.2
- visc_rate: float32 [4, 256, 256], P(None, 'space'), may hold values from 0.02 to 2
- fiber_stiff: float32 [4, 256, 256], P(None, 'space'), may hold values from 0.05 to 0.25
- fiber_family: int32 [64, 8], P('space'), may hold values from 0 to 3
- pressure: float32 [32, 4], P('tm'), may hold values from 0.2 to 1
Outputs:
- new_disp: float32 [32, 3, 4, 256, 256], P('tm', None, None, 'space')
- new_vel: float32 [32, 3, 4, 256, 256], P('tm', None, None, 'space')
- new_visc: float32 [32, 3, 4, 256, 256], P('tm', None, None, 'space')
The draws below stay inside these ranges and needn't reach their ends.
All inputs are finite; a program needn't handle non-finite values.
Results may differ from the reference program's by a relative error of at most 0.000029.
Values sent between devices are 32-bit elements; how exact they have to be, the bound alone decides.
A program may use at most 128 MiB of HBM per device.

```python
import math
import jax
import jax.numpy as jnp
from jax import lax

RAD = 4
CIR = 256
STEPS = 4
BLK_AX = 4
BLK_CIR = 32
NA = 256
SLABS = 32


def touch_ends(result, rng, low, high):
    place = [jax.random.randint(jax.random.fold_in(rng, axis), (), 0, length) for axis, length in enumerate(result.shape)]
    main_axis = result.shape.index(max(result.shape))
    beside = place[:main_axis] + [(place[main_axis] + 1) % result.shape[main_axis]] + place[main_axis + 1:]
    return result.at[tuple(place)].set(low).at[tuple(beside)].set(high)


def shard_levels(stream_key, extent, cuts, least, high):
    loudness, own = 1.0, jax.random.fold_in(stream_key, 6)
    for axis_at, parts in cuts:
        heights = jnp.exp(jax.random.uniform(jax.random.fold_in(own, axis_at), (parts,), jnp.float32, least / len(cuts), high / len(cuts)))
        loudness = loudness * jnp.repeat(heights, extent[axis_at] // parts).reshape([-1 if axis == axis_at else 1 for axis in range(len(extent))])
    return loudness


def normal_values(key, dims, scale, most, pieces=(), held_as=jnp.bfloat16):
    level = shard_levels(key, dims, pieces, -0.22, 0.18) if pieces else 1.0
    values = jax.random.normal(key, dims, jnp.float32) * scale * level
    return jnp.minimum(jnp.maximum(values, -most), most).astype(held_as)


def setup_inputs(seed: int = 0) -> dict:
    streams_of = jax.random.split(jax.random.key(seed), 11)
    return {
        "start_disp": normal_values(streams_of[0], (SLABS, 3, RAD, NA, CIR), 0.05, 0.2, ((0, 32), (3, 8)), jnp.float32),
        "start_vel": normal_values(streams_of[1], (SLABS, 3, RAD, NA, CIR), 0.05, 0.2, ((0, 32), (3, 8)), jnp.float32),
        "start_visc": normal_values(streams_of[2], (SLABS, 3, RAD, NA, CIR), 0.05, 0.2, ((0, 32), (3, 8)), jnp.float32),
        "init_state": normal_values(streams_of[3], (3, 3, RAD, NA, CIR), 0.05, 0.2, ((3, 8),), jnp.float32),
        "inv_mass": jnp.clip(jnp.exp(math.log(1.0) - 1.0498221 * jax.random.uniform(streams_of[4], (RAD, NA, CIR), jnp.float32) ** shard_levels(streams_of[4], (RAD, NA, CIR), ((1, 8),), -0.2, 0.2)), 0.35, 1.0),
        "damping_rate": jnp.clip(jnp.exp(math.log(0.2) - 4.6051702 * jax.random.uniform(streams_of[5], (RAD, NA, CIR), jnp.float32) ** shard_levels(streams_of[5], (RAD, NA, CIR), ((1, 8),), -0.2, 0.2)), 0.002, 0.2),
        "visc_rate": jnp.clip(jnp.exp(math.log(2.0) - 4.6051702 * jax.random.uniform(streams_of[6], (RAD, NA, CIR), jnp.float32) ** shard_levels(streams_of[6], (RAD, NA, CIR), ((1, 8),), -0.2, 0.2)), 0.02, 2.0),
        "fiber_stiff": jnp.clip(jnp.exp(math.log(0.25) - 1.609438 * jax.random.uniform(streams_of[7], (RAD, NA, CIR), jnp.float32) ** shard_levels(streams_of[7], (RAD, NA, CIR), ((1, 8),), -0.2, 0.2)), 0.05, 0.25),
        "fiber_family": touch_ends(jax.random.randint(streams_of[8], (NA // BLK_AX, CIR // BLK_CIR), 0, 4), jax.random.fold_in(streams_of[8], 1), 0, 3).astype(jnp.int32),
        "pressure": jnp.clip(jnp.exp(math.log(1.0) - 1.609438 * jax.random.uniform(streams_of[9], (SLABS, STEPS), jnp.float32) ** shard_levels(streams_of[9], (SLABS, STEPS), ((0, 32),), -0.2, 0.2)), 0.2, 1.0),
    }


COEF_AXIAL = 0.22
COEF_CIRC = 0.22
COEF_RADIAL = 0.12
VISC_SHARE = 0.6
TIME_STEP = 1.0
FIBER_ANGLES = (0.5, -0.5, 0.9, -0.9)


def directions(fiber_family, block_rows, block_cols):
    count_a, count_c = fiber_family.shape
    spread = jnp.broadcast_to(fiber_family[:, None, :, None], (count_a, block_rows, count_c, block_cols))
    spread = spread.reshape(count_a * block_rows, count_c * block_cols)
    cosine = jnp.zeros(spread.shape, jnp.float32)
    sine_part = jnp.zeros(spread.shape, jnp.float32)
    for family, radians in enumerate(FIBER_ANGLES):
        chosen = jnp.where(spread == family, 1.0, 0.0).astype(jnp.float32)
        cosine = cosine + chosen * math.cos(radians)
        sine_part = sine_part + chosen * math.sin(radians)
    return cosine, sine_part


def materials(fiber_stiff, fiber_family):
    cosine, sine_part = directions(fiber_family, BLK_AX, BLK_CIR)
    return jnp.stack([fiber_stiff, jnp.broadcast_to(cosine, fiber_stiff.shape), jnp.broadcast_to(sine_part, fiber_stiff.shape)])


def pad_axial(field):
    return jnp.pad(field, ((0, 0), (0, 0), (1, 1), (0, 0)))


def stencil(u_pad, mat_pad):
    center = u_pad[:, :, 1:-1]
    axial = u_pad[:, :, 2:] + u_pad[:, :, :-2] - 2.0 * center
    circle = jnp.roll(center, 1, 3) + jnp.roll(center, -1, 3) - 2.0 * center
    radial_pad = jnp.pad(center, ((0, 0), (1, 1), (0, 0), (0, 0)))
    radial = radial_pad[:, 2:] + radial_pad[:, :-2] - 2.0 * center
    elastic = COEF_AXIAL * axial + COEF_CIRC * circle + COEF_RADIAL * radial
    grad_axial = u_pad[:, :, 1:] - u_pad[:, :, :-1]
    lower = u_pad[:, :, :-1]
    grad_circ = jnp.roll(lower, -1, 3) - lower
    stiffness = mat_pad[0, :, :-1]
    cosine = mat_pad[1, :, :-1]
    sine_part = mat_pad[2, :, :-1]
    strain = cosine * cosine * grad_axial[1] + sine_part * sine_part * grad_circ[2] + cosine * sine_part * (grad_axial[2] + grad_circ[1])
    weight = jnp.exp(strain * strain)
    sigma = stiffness * weight * strain
    axial_one = sigma * cosine * cosine
    mixed = sigma * cosine * sine_part
    circ_two = sigma * sine_part * sine_part
    own_mixed = mixed[:, 1:]
    own_circ = circ_two[:, 1:]
    force_one = (axial_one[:, 1:] - axial_one[:, :-1]) + (own_mixed - jnp.roll(own_mixed, 1, 2))
    force_two = (mixed[:, 1:] - mixed[:, :-1]) + (own_circ - jnp.roll(own_circ, 1, 2))
    fiber = jnp.stack([jnp.zeros_like(force_one), force_one, force_two])
    return elastic + fiber, elastic, weight[:, 1:]


def fine_step(state, u_pad, mat_pad, inv_mass, damping_rate, decay_factor, pressure_now):
    displace, velocity, viscous = state
    force_total, elastic, weight = stencil(u_pad, mat_pad)
    inner_wall = jnp.zeros((3, displace.shape[1], 1, 1), jnp.float32).at[0, 0].set(1.0)
    load_total = force_total + viscous + pressure_now * inner_wall
    acceleration = inv_mass * load_total - damping_rate * velocity
    next_vel = velocity + TIME_STEP * acceleration
    next_disp = displace + TIME_STEP * next_vel
    next_visc = decay_factor * viscous + (1.0 - decay_factor) * VISC_SHARE * elastic
    return (next_disp, next_vel, next_visc), weight


def coarse_matrix(inv_mass, damping_rate, fiber_stiff, weight):
    half_step = 0.5 * STEPS * TIME_STEP
    stiffness = inv_mass * (2.0 * (COEF_AXIAL + COEF_CIRC + COEF_RADIAL) + 2.0 * fiber_stiff * weight)
    damping_part = half_step * damping_rate
    square_part = half_step * half_step * stiffness
    determinant = 1.0 + damping_part + square_part
    return jnp.stack([(1.0 + damping_part - square_part) / determinant, (2.0 * half_step) / determinant, -2.0 * half_step * stiffness / determinant, (1.0 - damping_part - square_part) / determinant])


def relax(start, mat_pad, inv_mass, damping_rate, decay_factor, fiber_stiff, pressure_row, pad_field):
    state = start
    first_weight = None
    for section in range(STEPS):
        u_pad = pad_field(state[0])
        state, weight = fine_step(state, u_pad, mat_pad, inv_mass, damping_rate, decay_factor, pressure_row[section])
        if section == 0:
            first_weight = weight
    return state, coarse_matrix(inv_mass, damping_rate, fiber_stiff, first_weight)


def reference(start_disp, start_vel, start_visc, init_state, inv_mass, damping_rate, visc_rate, fiber_stiff, fiber_family, pressure):
    mat_pad = pad_axial(materials(fiber_stiff, fiber_family))
    decay_factor = jnp.exp(-TIME_STEP * visc_rate)

    def one_slab(slab):
        displace, velocity, viscous, pressure_row = slab
        state, gmat = relax((displace, velocity, viscous), mat_pad, inv_mass, damping_rate, decay_factor, fiber_stiff, pressure_row, pad_axial)
        return state[0], state[1], state[2], gmat

    end_disp, end_vel, end_visc, gmats = lax.map(one_slab, (start_disp, start_vel, start_visc, pressure))
    prior_disp = jnp.concatenate([init_state[0][None], end_disp[:-1]], 0)
    prior_vel = jnp.concatenate([init_state[1][None], end_vel[:-1]], 0)
    prior_visc = jnp.concatenate([init_state[2][None], end_visc[:-1]], 0)
    resid_disp = prior_disp - start_disp
    resid_vel = prior_vel - start_vel

    def chain(carried, inputs):
        error_disp, error_vel = carried
        gmat, part_disp, part_vel = inputs
        sum_disp = error_disp + part_disp
        sum_vel = error_vel + part_vel
        next_disp = gmat[0] * sum_disp + gmat[1] * sum_vel
        next_vel = gmat[2] * sum_disp + gmat[3] * sum_vel
        return (next_disp, next_vel), (error_disp, error_vel)

    zero_field = jnp.zeros(start_disp.shape[1:], jnp.float32)
    _, (errors_disp, errors_vel) = lax.scan(chain, (zero_field, zero_field), (gmats, resid_disp, resid_vel))
    return prior_disp + errors_disp, prior_vel + errors_vel, prior_visc
```

```python
import functools
import math

import jax
import jax.numpy as jnp
from jax import lax
from jax.experimental import pallas as pl
from jax.experimental.pallas import tpu as pltpu
from jax.sharding import PartitionSpec as P

MESH = pl.DeviceIdType.MESH
STEPS = 4
BLK_CIR = 32
AX = 0.22
RA = 0.12
CENTER = 2.0 * (AX + AX + RA)
SHARE = 0.6
F32 = jnp.float32
CHIPS = 16

INNER = (0, 4)
OUTER = (4, 7)


def expand(fam):
    col = lax.broadcasted_iota(jnp.int32, (8, 256), 1) // BLK_CIR
    row = lax.broadcasted_iota(jnp.int32, (8, 256), 0)
    return jnp.dot(
        fam.astype(F32), (col == row).astype(F32), preferred_element_type=F32
    )


def gmatrix(w, im, dp, fs):
    k = im * (CENTER + 2.0 * fs * w)
    hc = 2.0 * dp
    hk = 4.0 * k
    inv = 1.0 / (1.0 + hc + hk)
    return ((1.0 + hc - hk) * inv, 4.0 * inv, -hk * inv, (1.0 - hc - hk) * inv)


def kernel(
    sd, sv, sq, ini, im, dp, vr, fs, fam, prs,
    o_d, o_v, o_q,
    U, V, Q, M, T, SG, WT, FM, IT, Y, Z, S, R, B, NR, E, QE,
    ld, hs, hr, xs, xr, fsd, frc, bs, br, es, er, qs, qr,
):
    t = lax.axis_index("tm")
    sp = lax.axis_index("space")
    me = t // 2
    a = t % 2
    buddy = {"tm": me * 2 + (1 - a)}
    half = pl.ds(pl.multiple_of(a * 128, 128), 128)
    other = pl.ds(pl.multiple_of((1 - a) * 128, 128), 128)

    loads = []

    def load(src, dst):
        c = pltpu.make_async_copy(src, dst, ld.at[len(loads)])
        c.start()
        loads.append(c)

    for slot, src in ((slice(0, 4), slice(0, 4)), (4, 3), (6, 0)):
        load(sd.at[:, :, src], U.at[0, :, pl.ds(1, 4), slot])
        load(sv.at[:, src], V.at[0, :, slot])
        load(sq.at[:, src], Q.at[:, slot])
        for i, m in enumerate((im, dp, vr, fs)):
            load(m.at[:, src], M.at[i, :, slot])
    load(fam, FM.at[0])
    rad_m, g_m = me // 4, me % 4
    load(ini.at[pl.ds(0, 6), rad_m, g_m], IT)

    bar = pltpu.get_barrier_semaphore()

    def greet(k, _):
        d = lax.rem(me + k, CHIPS)
        pl.semaphore_signal(bar, inc=1, device_id={"tm": d * 2 + a}, device_id_type=MESH)
        return 0

    lax.fori_loop(1, CHIPS, greet, 0)
    pl.semaphore_signal(bar, inc=1, device_id=buddy, device_id_type=MESH)
    chain = jnp.logical_or(
        jnp.logical_and(a == 1, t < 31), jnp.logical_and(a == 0, t > 0)
    )
    mate = {"tm": jnp.where(a == 1, t + 1, t - 1)}

    @pl.when(chain)
    def _():
        pl.semaphore_signal(bar, inc=1, device_id=mate, device_id_type=MESH)

    @pl.when(sp > 0)
    def _():
        pl.semaphore_signal(bar, inc=1, device_id={"space": sp - 1}, device_id_type=MESH)

    @pl.when(sp < 7)
    def _():
        pl.semaphore_signal(bar, inc=1, device_id={"space": sp + 1}, device_id_type=MESH)

    zero = jnp.zeros((8, 256), F32)

    def clear(i, _):
        for s in range(STEPS):
            for c in range(3):
                U[s, c, 0, i] = zero
                U[s, c, 5, i] = zero
        return 0

    lax.fori_loop(0, 7, clear, 0)

    for edge, rows in ((7, slice(0, 4)), (0, slice(4, 8))):

        @pl.when(sp == edge)
        def _(rows=rows):
            blank = jnp.zeros((4, 256), F32)
            for c in range(3):
                for r in range(4):
                    U[0, c, r + 1, 5, rows] = blank
                    V[0, c * 4 + r, 5, rows] = blank
                    Q[c * 4 + r, 5, rows] = blank
            for i in range(4):
                for r in range(4):
                    M[i, r, 5, rows] = blank

    greeted = 16 + jnp.where(chain, 1, 0) + jnp.where(sp > 0, 1, 0) + jnp.where(sp < 7, 1, 0)
    pl.semaphore_wait(bar, greeted)

    def halo(side):
        grp, rows, to = ((0, pl.ds(0, 4), sp - 1), (3, pl.ds(4, 4), sp + 1))[side]
        pairs = [
            (sd.at[:, :, grp, rows], U.at[0, :, pl.ds(1, 4), 5, rows]),
            (sv.at[:, grp, rows], V.at[0, :, 5, rows]),
            (sq.at[:, grp, rows], Q.at[:, 5, rows]),
        ]
        for i, m in enumerate((im, dp, vr, fs)):
            pairs.append((m.at[:, grp, rows], M.at[i, :, 5, rows]))
        pairs.append((fam, FM.at[1 + side]))
        return [
            pltpu.make_async_remote_copy(
                src_ref=src, dst_ref=dst, send_sem=hs.at[side, i], recv_sem=hr.at[side, i],
                device_id={"space": to}, device_id_type=MESH,
            )
            for i, (src, dst) in enumerate(pairs)
        ]

    has_from = (sp < 7, sp > 0)
    has_to = (sp > 0, sp < 7)
    for side in (0, 1):

        @pl.when(has_to[side])
        def _(side=side):
            for c in halo(side):
                c.start()

    for c in loads:
        c.wait()

    sub = lax.broadcasted_iota(jnp.int32, (8, 256), 0)

    def following(x, n):
        return jnp.where(sub == 7, pltpu.roll(n, 7, 0), pltpu.roll(x, 7, 0))

    def preceding(x, p):
        return jnp.where(sub == 0, pltpu.roll(p, 1, 0), pltpu.roll(x, 1, 0))

    def after(x):
        return pltpu.roll(x, 255, 1)

    def before(x):
        return pltpu.roll(x, 1, 1)

    def angles(slot, first, second):
        f = jnp.where(
            sub < 4, jnp.broadcast_to(first, (8, 256)), jnp.broadcast_to(second, (8, 256))
        )
        wide = f > 1.5
        co = jnp.where(wide, math.cos(0.9), math.cos(0.5)).astype(F32)
        si = jnp.where(wide, math.sin(0.9), math.sin(0.5)).astype(F32)
        odd = jnp.where(wide, f - 2.0, f) > 0.5
        si = jnp.where(odd, -si, si)
        T[0, slot] = co * co
        T[1, slot] = co * si
        T[2, slot] = si * si

    def prepare(lo, hi):
        for p in range(lo, hi):
            b = hi - 1 if p == lo else p - 1
            T[3, p] = preceding(T[0, p], T[0, b])
            T[4, p] = preceding(T[1, p], T[1, b])
            T[5, p] = before(T[1, p])
            T[6, p] = before(T[2, p])

        def decay(p, _):
            for r in range(4):
                M[2, r, p] = jnp.exp(-M[2, r, p])
            return 0

        lax.fori_loop(lo, hi, decay, 0)

    def steps(lo, hi):
        def strains(s, p):
            n = jnp.where(p == hi - 1, lo, p + 1)
            co2, cs, si2 = T[0, p], T[1, p], T[2, p]
            for r in range(4):
                u1 = U[s, 1, r + 1, p]
                u2 = U[s, 2, r + 1, p]
                d1 = following(u1, U[s, 1, r + 1, n]) - u1
                d2 = following(u2, U[s, 2, r + 1, n]) - u2
                e = co2 * d1 + si2 * (after(u2) - u2) + cs * (d2 + (after(u1) - u1))
                w = jnp.exp(e * e)
                SG[r, p] = M[3, r, p] * w * e

                @pl.when(s == 0)
                def _(r=r, w=w):
                    WT[r, p] = w

        def advance(s, p):
            n = jnp.where(p == hi - 1, lo, p + 1)
            b = jnp.where(p == lo, hi - 1, p - 1)
            co2, cs, si2 = T[0, p], T[1, p], T[2, p]
            co2b, csb, csc, si2c = T[3, p], T[4, p], T[5, p], T[6, p]
            for r in range(4):
                sg = SG[r, p]
                sga = preceding(sg, SG[r, b])
                sgc = before(sg)
                force = (
                    None,
                    (co2 * sg - co2b * sga) + (cs * sg - csc * sgc),
                    (cs * sg - csb * sga) + (si2 * sg - si2c * sgc),
                )
                mass, damp, d = M[0, r, p], M[1, r, p], M[2, r, p]
                gain = SHARE * (1.0 - d)
                for c in range(3):
                    u = U[s, c, r + 1, p]
                    near = (
                        following(u, U[s, c, r + 1, n])
                        + preceding(u, U[s, c, r + 1, b])
                        + after(u)
                        + before(u)
                    )
                    el = (
                        AX * near
                        + RA * (U[s, c, r, p] + U[s, c, r + 2, p])
                        - CENTER * u
                    )
                    i = c * 4 + r
                    q = Q[i, p]
                    total = el + q
                    if c:
                        total = total + force[c]
                    elif r == 0:
                        total = total + prs[0, s]
                    v = V[s, i, p]
                    v = v + mass * total - damp * v
                    V[s + 1, i, p] = v
                    U[s + 1, c, r + 1, p] = u + v
                    Q[i, p] = d * q + gain * el

        def one(s, _):
            lax.fori_loop(lo, hi, lambda p, _: (strains(s, p), 0)[1], 0)
            lax.fori_loop(lo, hi, lambda p, _: (advance(s, p), 0)[1], 0)
            return 0

        lax.fori_loop(0, STEPS, one, 0)

    spread = expand(FM[0])
    for g in range(4):
        angles(g, spread[2 * g : 2 * g + 1], spread[2 * g + 1 : 2 * g + 2])
    prepare(*INNER)
    steps(*INNER)

    def joined(g, get):
        if g == 0:
            return jnp.where(sub < 4, get(6), get(0))
        if g == 3:
            return jnp.where(sub < 4, get(3), get(4))
        return get(g)

    def swap(d):
        return pltpu.make_async_remote_copy(
            src_ref=Z.at[d], dst_ref=Y.at[a, d], send_sem=xs.at[d], recv_sem=xr.at[d],
            device_id=buddy, device_id_type=MESH,
        )

    def swapped(d):
        return pltpu.make_async_remote_copy(
            src_ref=Z.at[d], dst_ref=Y.at[1 - a, d], send_sem=xs.at[d], recv_sem=xr.at[d],
            device_id=buddy, device_id_type=MESH,
        )

    first = a == 0

    def maps(g):
        for r in range(4):
            d = r * 4 + g

            def put(j, x, d=d):
                x0, x1 = x[:, :128], x[:, 128:]
                Y[a, d, j] = jnp.where(first, x0, x1)
                Z[d, j] = jnp.where(first, x1, x0)

            w = joined(g, lambda k, r=r: WT[r, k])
            g00, g01, g10, g11 = gmatrix(w, M[0, r, g], M[1, r, g], M[3, r, g])
            put(6, w)
            for c in range(3):
                i = c * 4 + r
                u0, v0 = U[0, c, r + 1, g], V[0, i, g]
                u4 = joined(g, lambda k, c=c, r=r: U[STEPS, c, r + 1, k])
                v4 = joined(g, lambda k, i=i: V[STEPS, i, k])
                put(c, u4 - (g00 * u0 + g01 * v0))
                put(3 + c, v4 - (g10 * u0 + g11 * v0))
                QE[c, r, g] = joined(g, lambda k, i=i: Q[i, k])
            swap(d).start()

    def onward(d):
        return pltpu.make_async_remote_copy(
            src_ref=S.at[d], dst_ref=R.at[me], send_sem=fsd.at[d], recv_sem=frc.at[me],
            device_id={"tm": d * 2 + a}, device_id_type=MESH,
        )

    def compose(early):
        def tile(k, _):
            d = lax.rem(me + k, CHIPS)

            @pl.when((lax.rem((d + 1) // 2, 2) == 1) == early)
            def _():
                swapped(d).wait_recv()
                r, g = d // 4, d % 4
                w1 = Y[1, d, 6]
                g00, g01, g10, g11 = gmatrix(
                    w1, M[0, r, g, :, half], M[1, r, g, :, half], M[3, r, g, :, half]
                )
                S[d, 6] = Y[0, d, 6]
                S[d, 7] = w1
                for c in range(3):
                    cu, cv = Y[0, d, c], Y[0, d, 3 + c]
                    S[d, c] = g00 * cu + g01 * cv + Y[1, d, c]
                    S[d, 3 + c] = g10 * cu + g11 * cv + Y[1, d, 3 + c]

                @pl.when(d != me)
                def _():
                    onward(d).start()

            return 0

        lax.fori_loop(0, CHIPS, tile, 0)

    maps(1)
    maps(2)

    for side in (0, 1):

        @pl.when(has_from[side])
        def _(side=side):
            for c in halo(side):
                c.wait_recv()

    compose(True)

    after_row = expand(FM[1])[0:1]
    before_row = expand(FM[2])[7:8]
    angles(4, spread[6:7], spread[7:8])
    angles(5, after_row, before_row)
    angles(6, spread[0:1], spread[1:2])
    prepare(*OUTER)
    steps(*OUTER)
    maps(0)
    maps(3)
    compose(False)

    def pass_q(to):
        return pltpu.make_async_remote_copy(
            src_ref=QE, dst_ref=o_q, send_sem=qs, recv_sem=qr,
            device_id={"tm": to}, device_id_type=MESH,
        )

    @pl.when(t < 31)
    def _():
        pass_q(t + 1).start()

    @pl.when(t == 0)
    def _():
        c = pltpu.make_async_copy(ini.at[pl.ds(6, 3)], o_q, ld.at[0])
        c.start()
        c.wait()

    mine = [M[i, rad_m, g_m, :, half] for i in (0, 1, 3)]

    def back(c):
        return pltpu.make_async_remote_copy(
            src_ref=B.at[c], dst_ref=NR.at[me], send_sem=bs.at[c], recv_sem=br.at[me],
            device_id={"tm": c * 2 + a}, device_id_type=MESH,
        )

    def arrived_f(c):
        return pltpu.make_async_remote_copy(
            src_ref=S.at[c], dst_ref=R.at[c], send_sem=fsd.at[c], recv_sem=frc.at[c],
            device_id={"tm": c * 2 + a}, device_id_type=MESH,
        )

    def arrived_b(c):
        return pltpu.make_async_remote_copy(
            src_ref=B.at[c], dst_ref=NR.at[c], send_sem=bs.at[c], recv_sem=br.at[c],
            device_id={"tm": c * 2 + a}, device_id_type=MESH,
        )

    for j in range(8):
        R[me, j] = S[me, j]

    def chip(c, now):
        for j in range(6):
            B[c, j] = now[j]

        @pl.when(c != me)
        def _():
            back(c).start()
            arrived_f(c).wait_recv()

        ga = gmatrix(R[c, 6], *mine)
        gb = gmatrix(R[c, 7], *mine)
        us, vs = [], []
        for j in range(3):
            u, v = now[j], now[3 + j]
            u, v = ga[0] * u + ga[1] * v, ga[2] * u + ga[3] * v
            us.append(gb[0] * u + gb[1] * v + R[c, j])
            vs.append(gb[2] * u + gb[3] * v + R[c, 3 + j])
        return tuple(us + vs)

    lax.fori_loop(0, CHIPS, chip, tuple(IT[j, :, half] for j in range(6)))
    for j in range(6):
        NR[me, j] = B[me, j]

    def deliver(d, field):
        out = (o_d, o_v)[field]
        return pltpu.make_async_remote_copy(
            src_ref=E.at[d, pl.ds(3 * field, 3)], dst_ref=out.at[:, d // 4, d % 4, :, half],
            send_sem=es.at[field, d], recv_sem=er.at[field, d],
            device_id=buddy, device_id_type=MESH,
        )

    def delivered(d, field):
        out = (o_d, o_v)[field]
        return pltpu.make_async_remote_copy(
            src_ref=E.at[d, pl.ds(3 * field, 3)], dst_ref=out.at[:, d // 4, d % 4, :, other],
            send_sem=es.at[field, d], recv_sem=er.at[field, d],
            device_id=buddy, device_id_type=MESH,
        )

    def finish(k, _):
        d = lax.rem(me + k, CHIPS)

        @pl.when(d != me)
        def _():
            arrived_b(d).wait_recv()

        r, g = d // 4, d % 4
        ga = gmatrix(
            Y[0, d, 6], M[0, r, g, :, half], M[1, r, g, :, half], M[3, r, g, :, half]
        )
        for j in range(3):
            u, v = NR[d, j], NR[d, 3 + j]
            u1 = ga[0] * u + ga[1] * v + Y[0, d, j]
            v1 = ga[2] * u + ga[3] * v + Y[0, d, 3 + j]
            E[d, j] = jnp.where(first, u1, u)
            E[d, 3 + j] = jnp.where(first, v1, v)
            o_d[j, r, g, :, half] = jnp.where(first, u, u1)
            o_v[j, r, g, :, half] = jnp.where(first, v, v1)
        deliver(d, 0).start()
        deliver(d, 1).start()
        return 0

    lax.fori_loop(0, CHIPS, finish, 0)

    def settle(d, _):
        for f in (0, 1):
            delivered(d, f).wait_recv()
            deliver(d, f).wait_send()
        swap(d).wait_send()

        @pl.when(d != me)
        def _():
            onward(d).wait_send()
            back(d).wait_send()

        return 0

    lax.fori_loop(0, CHIPS, settle, 0)
    for side in (0, 1):

        @pl.when(has_to[side])
        def _(side=side):
            for c in halo(side):
                c.wait_send()

    @pl.when(t < 31)
    def _():
        pass_q(t + 1).wait_send()

    @pl.when(t > 0)
    def _():
        pass_q(t).wait_recv()


def step(
    start_disp, start_vel, start_visc, init_state, inv_mass, damping_rate, visc_rate,
    fiber_stiff, fiber_family, pressure,
):
    any_ = pl.BlockSpec(memory_space=pl.ANY)
    vmem = pl.BlockSpec(memory_space=pltpu.VMEM)
    out = jax.ShapeDtypeStruct((3, 4, 4, 8, 256), F32)
    dma = pltpu.SemaphoreType.DMA
    outs = pl.pallas_call(
        kernel,
        out_shape=(out, out, out),
        in_specs=[any_] * 9 + [pl.BlockSpec(memory_space=pltpu.SMEM)],
        out_specs=(vmem, vmem, vmem),
        scratch_shapes=[
            pltpu.VMEM((STEPS + 1, 3, 6, 7, 8, 256), F32),
            pltpu.VMEM((STEPS + 1, 12, 7, 8, 256), F32),
            pltpu.VMEM((12, 7, 8, 256), F32),
            pltpu.VMEM((4, 4, 7, 8, 256), F32),
            pltpu.VMEM((7, 7, 8, 256), F32),
            pltpu.VMEM((4, 7, 8, 256), F32),
            pltpu.VMEM((4, 7, 8, 256), F32),
            pltpu.VMEM((3, 8, 8), jnp.int32),
            pltpu.VMEM((6, 8, 256), F32),
            pltpu.VMEM((2, 16, 7, 8, 128), F32),
            pltpu.VMEM((16, 7, 8, 128), F32),
            pltpu.VMEM((16, 8, 8, 128), F32),
            pltpu.VMEM((16, 8, 8, 128), F32),
            pltpu.VMEM((16, 6, 8, 128), F32),
            pltpu.VMEM((16, 6, 8, 128), F32),
            pltpu.VMEM((16, 6, 8, 128), F32),
            pltpu.VMEM((3, 4, 4, 8, 256), F32),
            dma((24,)), dma((2, 8)), dma((2, 8)), dma((16,)), dma((16,)), dma((16,)), dma((16,)),
            dma((16,)), dma((16,)), dma((2, 16)), dma((2, 16)), dma(()), dma(()),
        ],
        compiler_params=pltpu.CompilerParams(
            collective_id=0, has_side_effects=True, vmem_limit_bytes=40 * 1024 * 1024
        ),
    )(
        start_disp.reshape(3, 4, 4, 8, 256),
        start_vel.reshape(12, 4, 8, 256),
        start_visc.reshape(12, 4, 8, 256),
        init_state.reshape(9, 4, 4, 8, 256),
        inv_mass.reshape(4, 4, 8, 256),
        damping_rate.reshape(4, 4, 8, 256),
        visc_rate.reshape(4, 4, 8, 256),
        fiber_stiff.reshape(4, 4, 8, 256),
        fiber_family,
        pressure,
    )
    return tuple(x.reshape(1, 3, 4, 32, 256) for x in outs)


def solution(mesh):
    state = P("tm", None, None, "space", None)
    cell = P(None, "space", None)
    return jax.shard_map(
        step,
        mesh=mesh,
        in_specs=(
            state, state, state, P(None, None, None, "space", None),
            cell, cell, cell, cell, P("space", None), P("tm", None),
        ),
        out_specs=(state, state, state),
        check_vma=False,
    )
```

```python
import functools
import math

import jax
import jax.numpy as jnp
from jax import lax
from jax.experimental import pallas as pl
from jax.experimental.pallas import tpu as pltpu
from jax.sharding import PartitionSpec as P

MESH = pl.DeviceIdType.MESH
STEPS = 4
BLK_CIR = 32
AX = 0.22
RA = 0.12
CENTER = 2.0 * (AX + AX + RA)
SHARE = 0.6
F32 = jnp.float32
CHIPS = 16

ROWS = 80
INNER = (1, 5)
OUTER = (6, 9)
EARLY = (0, 6)
LATE = (6, 2)


def expand(fam):
    col = lax.broadcasted_iota(jnp.int32, (8, 256), 1) // BLK_CIR
    row = lax.broadcasted_iota(jnp.int32, (8, 256), 0)
    return jnp.dot(
        fam.astype(F32), (col == row).astype(F32), preferred_element_type=F32
    )


def gmatrix(w, im, dp, fs):
    k = im * (CENTER + 2.0 * fs * w)
    hc = 2.0 * dp
    hk = 4.0 * k
    inv = 1.0 / (1.0 + hc + hk)
    return ((1.0 + hc - hk) * inv, 4.0 * inv, -hk * inv, (1.0 - hc - hk) * inv)


def rows(p, shift=0):
    return pl.ds(8 * p + shift, 8)


def kernel(
    sd, sv, sq, ini, im, dp, vr, fs, fam, prs,
    o_d, o_v, o_q,
    U, V, Q, M, T, SG, W, FM, IT, IQ, PR, Y, Z, S, R, GG, B, NR, O, E,
    ld, hs, hr, xs, xr, fsd, frc, bs, br, es, er, qs, qr, os,
):
    t = lax.axis_index("tm")
    sp = lax.axis_index("space")
    me = t // 2
    a = t % 2
    first = a == 0
    buddy = {"tm": me * 2 + (1 - a)}
    lanes = (pl.ds(0, 128), pl.ds(128, 128))

    loads = []

    def load(src, dst):
        c = pltpu.make_async_copy(src, dst, ld.at[len(loads)])
        c.start()
        loads.append(c)

    states = ((sd, lambda *i: U.at[(0,) + i]), (sv, lambda *i: V.at[(0,) + i]), (sq, lambda *i: Q.at[i]))
    mats = tuple((m, lambda *i, k=k: M.at[(k,) + i]) for k, m in enumerate((im, dp, vr, fs)))
    fields = states + mats
    every = slice(None)
    for h in (0, 1):
        for src, dst in fields:
            load(src.at[:, :, lanes[h]], dst(every, h, pl.ds(8, 32)))
            load(src.at[:, pl.ds(24, 8), lanes[h]], dst(every, h, pl.ds(48, 8)))
            load(src.at[:, pl.ds(0, 8), lanes[h]], dst(every, h, pl.ds(64, 8)))
    load(fam, FM.at[0])
    load(prs, PR)
    rad_m, q_m = me // 4, me % 4
    for h in (0, 1):
        load(ini.at[pl.ds(0, 6), rad_m, :, lanes[h]], IT.at[:, h])

    bar = pltpu.get_barrier_semaphore()

    def greet(k, _):
        d = lax.rem(me + k, CHIPS)
        pl.semaphore_signal(bar, inc=1, device_id={"tm": d * 2 + a}, device_id_type=MESH)
        return 0

    @pl.when(sp > 0)
    def _():
        pl.semaphore_signal(bar, inc=1, device_id={"space": sp - 1}, device_id_type=MESH)

    @pl.when(sp < 7)
    def _():
        pl.semaphore_signal(bar, inc=1, device_id={"space": sp + 1}, device_id_type=MESH)

    lax.fori_loop(1, CHIPS, greet, 0)
    pl.semaphore_signal(bar, inc=1, device_id=buddy, device_id_type=MESH)
    chain = jnp.logical_or(
        jnp.logical_and(a == 1, t < 31), jnp.logical_and(a == 0, t > 0)
    )
    mate = {"tm": jnp.where(a == 1, t + 1, t - 1)}

    @pl.when(chain)
    def _():
        pl.semaphore_signal(bar, inc=1, device_id=mate, device_id_type=MESH)

    for edge, at in ((7, pl.ds(56, 4)), (0, pl.ds(60, 4))):

        @pl.when(sp == edge)
        def _(at=at):
            blank = jnp.zeros((4, 128), F32)
            for h in (0, 1):
                for i in range(12):
                    U[0, i, h, at] = blank
                    V[0, i, h, at] = blank
                    Q[i, h, at] = blank
                for k in range(4):
                    for r in range(4):
                        M[k, r, h, at] = blank

    greeted = 16 + jnp.where(chain, 1, 0) + jnp.where(sp > 0, 1, 0) + jnp.where(sp < 7, 1, 0)
    pl.semaphore_wait(bar, greeted)

    def halo(side):
        cut, at, to = ((pl.ds(0, 4), pl.ds(56, 4), sp - 1), (pl.ds(28, 4), pl.ds(60, 4), sp + 1))[side]
        pairs = [(fam, FM.at[1 + side])]
        for src, dst in fields:
            for h in (0, 1):
                pairs.append((src.at[:, cut, lanes[h]], dst(every, h, at)))
        return [
            pltpu.make_async_remote_copy(
                src_ref=src, dst_ref=dst, send_sem=hs.at[side, i], recv_sem=hr.at[side, i],
                device_id={"space": to}, device_id_type=MESH,
            )
            for i, (src, dst) in enumerate(pairs)
        ]

    has_from = (sp < 7, sp > 0)
    has_to = (sp > 0, sp < 7)
    for side in (0, 1):

        @pl.when(has_to[side])
        def _(side=side):
            for c in halo(side):
                c.start()

    for c in loads:
        c.wait()

    lane = lax.broadcasted_iota(jnp.int32, (8, 128), 1)

    def after(x):
        y = [pltpu.roll(k, 127, 1) for k in x]
        return [jnp.where(lane == 127, y[1 - h], y[h]) for h in (0, 1)]

    def before(x):
        y = [pltpu.roll(k, 1, 1) for k in x]
        return [jnp.where(lane == 0, y[1 - h], y[h]) for h in (0, 1)]

    upper = lax.broadcasted_iota(jnp.int32, (8, 256), 0) < 4

    def angles(p, one, two):
        f = jnp.where(
            upper, jnp.broadcast_to(one, (8, 256)), jnp.broadcast_to(two, (8, 256))
        )
        wide = f > 1.5
        co = jnp.where(wide, math.cos(0.9), math.cos(0.5)).astype(F32)
        si = jnp.where(wide, math.sin(0.9), math.sin(0.5)).astype(F32)
        odd = jnp.where(wide, f - 2.0, f) > 0.5
        si = jnp.where(odd, -si, si)
        co2, cs, si2 = [[x[:, :128], x[:, 128:]] for x in (co * co, co * si, si * si)]
        csc, si2c = before(cs), before(si2)
        for h in (0, 1):
            T[0, h, rows(p)] = co2[h]
            T[1, h, rows(p)] = cs[h]
            T[2, h, rows(p)] = si2[h]
            T[3, h, rows(p)] = co2[h] + cs[h]
            T[4, h, rows(p)] = cs[h] + si2[h]
            T[5, h, rows(p)] = csc[h]
            T[6, h, rows(p)] = si2c[h]

    def prepare(lo, hi):
        def rates(p, _):
            for h in (0, 1):
                for r in range(4):
                    d = jnp.exp(-M[2, r, h, rows(p)])
                    M[2, r, h, rows(p)] = d
                    M[4, r, h, rows(p)] = 1.0 - M[1, r, h, rows(p)]
                    M[5, r, h, rows(p)] = SHARE * (1.0 - d)
            return 0

        lax.fori_loop(lo, hi, rates, 0)

    def both(f):
        return [f(0), f(1)]

    def strains(s, p):
        co2, cs, si2 = [both(lambda h, k=k: T[k, h, rows(p)]) for k in range(3)]
        for r in range(4):
            u1 = both(lambda h: U[s, 4 + r, h, rows(p)])
            u2 = both(lambda h: U[s, 8 + r, h, rows(p)])
            c1, c2 = after(u1), after(u2)
            for h in (0, 1):
                d1 = U[s, 4 + r, h, rows(p, 1)] - u1[h]
                d2 = U[s, 8 + r, h, rows(p, 1)] - u2[h]
                e = co2[h] * d1 + si2[h] * (c2[h] - u2[h]) + cs[h] * (d2 + (c1[h] - u1[h]))
                w = jnp.exp(e * e)
                SG[r, h, rows(p)] = M[3, r, h, rows(p)] * w * e

                @pl.when(s == 0)
                def _(w=w, r=r, h=h):
                    W[r, h, rows(p)] = w

    def advance(s, p):
        for r in range(4):
            sg = both(lambda h: SG[r, h, rows(p)])
            sc = before(sg)
            f1, f2 = [], []
            for h in (0, 1):
                sb = SG[r, h, rows(p, -1)]
                f1.append(
                    T[3, h, rows(p)] * sg[h] - T[0, h, rows(p, -1)] * sb - T[5, h, rows(p)] * sc[h]
                )
                f2.append(
                    T[4, h, rows(p)] * sg[h] - T[1, h, rows(p, -1)] * sb - T[6, h, rows(p)] * sc[h]
                )
            force = (None, f1, f2)
            mass, d, keep, gain = [both(lambda h, k=k: M[k, r, h, rows(p)]) for k in (0, 2, 4, 5)]
            for c in range(3):
                i = c * 4 + r
                u = both(lambda h: U[s, i, h, rows(p)])
                ca, cb = after(u), before(u)
                for h in (0, 1):
                    near = (U[s, i, h, rows(p, 1)] + U[s, i, h, rows(p, -1)]) + (ca[h] + cb[h])
                    radial = U[s, i - 1, h, rows(p)] if r > 0 else U[s, i + 1, h, rows(p)]
                    if 0 < r < 3:
                        radial = radial + U[s, i + 1, h, rows(p)]
                    el = AX * near + RA * radial - CENTER * u[h]
                    q = Q[i, h, rows(p)]
                    total = el + q
                    if c:
                        total = total + force[c][h]
                    elif r == 0:
                        total = total + PR[0, s]
                    v = keep[h] * V[s, i, h, rows(p)] + mass[h] * total
                    V[s + 1, i, h, rows(p)] = v
                    U[s + 1, i, h, rows(p)] = u[h] + v
                    Q[i, h, rows(p)] = d[h] * q + gain[h] * el

    def steps(lo, hi):
        def one(s, _):
            lax.fori_loop(lo, hi, lambda p, _: (strains(s, p), 0)[1], 0)
            lax.fori_loop(lo, hi, lambda p, _: (advance(s, p), 0)[1], 0)
            return 0

        lax.fori_loop(0, STEPS, one, 0)

    spread = expand(FM[0])
    for g in range(4):
        angles(1 + g, spread[2 * g : 2 * g + 1], spread[2 * g + 1 : 2 * g + 2])
    prepare(*INNER)
    steps(*INNER)

    def maps(p):
        for r in range(4):

            def put(j, x, r=r):
                Y[a, j, r, rows(p)] = jnp.where(first, x[0], x[1])
                Z[j, r, rows(p)] = jnp.where(first, x[1], x[0])

            w = both(lambda h: W[r, h, rows(p)])
            g = both(
                lambda h: gmatrix(
                    w[h], M[0, r, h, rows(p)], M[1, r, h, rows(p)], M[3, r, h, rows(p)]
                )
            )
            put(6, w)
            for c in range(3):
                i = c * 4 + r
                cu, cv = [], []
                for h in (0, 1):
                    u0, v0 = U[0, i, h, rows(p)], V[0, i, h, rows(p)]
                    cu.append(U[STEPS, i, h, rows(p)] - (g[h][0] * u0 + g[h][1] * v0))
                    cv.append(V[STEPS, i, h, rows(p)] - (g[h][2] * u0 + g[h][3] * v0))
                put(c, cu)
                put(3 + c, cv)

    stretches = (pl.ds(8, 32), pl.ds(48, 8), pl.ds(64, 8))

    def swap(i, slab):
        return pltpu.make_async_remote_copy(
            src_ref=Z.at[:, :, stretches[i]], dst_ref=Y.at[slab, :, :, stretches[i]],
            send_sem=xs.at[i], recv_sem=xr.at[i], device_id=buddy, device_id_type=MESH,
        )

    def place(part, q):
        if part is EARLY:
            return 12 + 6 * q, 4 + 6 * q
        return jnp.where(q < 2, 64 + 2 * q, 48 + 2 * q), jnp.where(q < 2, 2 * q, 24 + 2 * q)

    def mix(part):
        return 0 if part is EARLY else 1

    def onward(part, d, slot):
        at = pl.ds(*part)
        return pltpu.make_async_remote_copy(
            src_ref=S.at[d, :, at], dst_ref=R.at[slot, :, at],
            send_sem=fsd.at[mix(part), d], recv_sem=frc.at[mix(part), slot],
            device_id={"tm": d * 2 + a}, device_id_type=MESH,
        )

    def compose(part):
        lo, n = part

        def tile(k, _):
            d = lax.rem(me + k, CHIPS)
            r, q = d // 4, d % 4
            at = pl.ds(place(part, q)[0], n)
            w1 = Y[1, 6, r, at]
            g = gmatrix(w1, M[0, r, a, at], M[1, r, a, at], M[3, r, a, at])
            S[d, 6, lo : lo + n] = Y[0, 6, r, at]
            S[d, 7, lo : lo + n] = w1
            for c in range(3):
                cu, cv = Y[0, c, r, at], Y[0, 3 + c, r, at]
                S[d, c, lo : lo + n] = g[0] * cu + g[1] * cv + Y[1, c, r, at]
                S[d, 3 + c, lo : lo + n] = g[2] * cu + g[3] * cv + Y[1, 3 + c, r, at]

            @pl.when(d != me)
            def _():
                onward(part, d, me).start()

            return 0

        lax.fori_loop(1, CHIPS + 1, tile, 0)
        R[me, :, lo : lo + n] = S[me, :, lo : lo + n]

    lax.fori_loop(*INNER, lambda p, _: (maps(p), 0)[1], 0)
    swap(0, a).start()
    swap(0, 1 - a).wait_recv()
    compose(EARLY)

    for side in (0, 1):

        @pl.when(has_from[side])
        def _(side=side):
            for c in halo(side):
                c.wait_recv()

    after_row = expand(FM[1])[0:1]
    before_row = expand(FM[2])[7:8]
    angles(6, spread[6:7], spread[7:8])
    angles(7, after_row, before_row)
    angles(8, spread[0:1], spread[1:2])
    prepare(*OUTER)
    steps(*OUTER)
    lax.fori_loop(0, 2, lambda p, _: (maps(6 + 2 * p), 0)[1], 0)
    for i in (1, 2):
        swap(i, a).start()
    for i in (1, 2):
        swap(i, 1 - a).wait_recv()
    compose(LATE)

    def pass_q(to):
        made = []
        for src, dst, n in ((12, 4, 4), (16, 8, 16), (32, 24, 4), (52, 28, 4), (64, 0, 4)):
            for h in (0, 1):
                i = len(made)
                made.append(
                    pltpu.make_async_remote_copy(
                        src_ref=Q.at[:, h, pl.ds(src, n)], dst_ref=o_q.at[:, pl.ds(dst, n), lanes[h]],
                        send_sem=qs.at[i], recv_sem=qr.at[i], device_id={"tm": to}, device_id_type=MESH,
                    )
                )
        return made

    @pl.when(t < 31)
    def _():
        for c in pass_q(t + 1):
            c.start()

    def back(part, c, slot):
        at = pl.ds(*part)
        return pltpu.make_async_remote_copy(
            src_ref=B.at[c, :, at], dst_ref=NR.at[slot, :, at],
            send_sem=bs.at[mix(part), c], recv_sem=br.at[mix(part), slot],
            device_id={"tm": c * 2 + a}, device_id_type=MESH,
        )

    def recur(part):
        lo, n = part
        at = slice(lo, lo + n)
        work, own = place(part, q_m)
        mine = [M[i, rad_m, a, pl.ds(work, n)] for i in (0, 1, 3)]

        def absorb(k, _):
            c = lax.rem(me + k, CHIPS)

            @pl.when(c != me)
            def _():
                onward(part, c, c).wait_recv()

            ga = gmatrix(R[c, 6, at], *mine)
            gb = gmatrix(R[c, 7, at], *mine)
            GG[c, 0, at] = gb[0] * ga[0] + gb[1] * ga[2]
            GG[c, 1, at] = gb[0] * ga[1] + gb[1] * ga[3]
            GG[c, 2, at] = gb[2] * ga[0] + gb[3] * ga[2]
            GG[c, 3, at] = gb[2] * ga[1] + gb[3] * ga[3]
            return 0

        lax.fori_loop(1, CHIPS + 1, absorb, 0)

        def chip(c, now):
            for j in range(6):
                B[c, j, at] = now[j]

            @pl.when(c != me)
            def _():
                back(part, c, me).start()

            g = [GG[c, j, at] for j in range(4)]
            us = [g[0] * now[j] + g[1] * now[3 + j] + R[c, j, at] for j in range(3)]
            vs = [g[2] * now[j] + g[3] * now[3 + j] + R[c, 3 + j, at] for j in range(3)]
            return tuple(us + vs)

        lax.fori_loop(0, CHIPS, chip, tuple(IT[j, a, pl.ds(own, n)] for j in range(6)))
        NR[me, :, at] = B[me, :, at]

    def finish(part):
        lo, n = part
        at = slice(lo, lo + n)

        def tile(k, _):
            d = lax.rem(me + k, CHIPS)

            @pl.when(d != me)
            def _():
                back(part, d, d).wait_recv()

            r, q = d // 4, d % 4
            work, own = place(part, q)
            work, own = pl.ds(work, n), pl.ds(own, n)
            g = gmatrix(Y[0, 6, r, work], M[0, r, a, work], M[1, r, a, work], M[3, r, a, work])
            for j in range(3):
                u, v = NR[d, j, at], NR[d, 3 + j, at]
                u1 = g[0] * u + g[1] * v + Y[0, j, r, work]
                v1 = g[2] * u + g[3] * v + Y[0, 3 + j, r, work]
                E[j, r, own] = jnp.where(first, u1, u)
                E[3 + j, r, own] = jnp.where(first, v1, v)
                O[j, r, a, own] = jnp.where(first, u, u1)
                O[3 + j, r, a, own] = jnp.where(first, v, v1)
            return 0

        lax.fori_loop(1, CHIPS + 1, tile, 0)

    spans = (pl.ds(8, 16), pl.ds(0, 8), pl.ds(24, 8))

    def deliver(i, h):
        return pltpu.make_async_remote_copy(
            src_ref=E.at[:, :, spans[i]], dst_ref=O.at[:, :, h, spans[i]],
            send_sem=es.at[i], recv_sem=er.at[i], device_id=buddy, device_id_type=MESH,
        )

    recur(EARLY)
    recur(LATE)

    @pl.when(t == 0)
    def _():
        c = pltpu.make_async_copy(ini.at[pl.ds(6, 3)], IQ, ld.at[0])
        c.start()
        c.wait()
        c = pltpu.make_async_copy(IQ, o_q.reshape(3, 4, 32, 256), ld.at[0])
        c.start()
        c.wait()

    finish(EARLY)
    deliver(0, a).start()
    finish(LATE)
    for i in (1, 2):
        deliver(i, a).start()

    def write(f, h, at):
        out = (o_d, o_v)[f]
        return pltpu.make_async_copy(
            O.at[pl.ds(3 * f, 3), :, h], out.at[:, :, :, at], os.at[f, h]
        )

    near = pl.ds(pl.multiple_of(a * 128, 128), 128)
    far = pl.ds(pl.multiple_of((1 - a) * 128, 128), 128)
    for f in (0, 1):
        write(f, a, near).start()
    for i in (0, 1, 2):
        deliver(i, 1 - a).wait_recv()
    for f in (0, 1):
        write(f, 1 - a, far).start()

    def settle(d, _):
        @pl.when(d != me)
        def _():
            for part in (EARLY, LATE):
                onward(part, d, me).wait_send()
                back(part, d, me).wait_send()

        return 0

    lax.fori_loop(0, CHIPS, settle, 0)
    for i in (0, 1, 2):
        swap(i, a).wait_send()
        deliver(i, a).wait_send()
    for side in (0, 1):

        @pl.when(has_to[side])
        def _(side=side):
            for c in halo(side):
                c.wait_send()

    @pl.when(t < 31)
    def _():
        for c in pass_q(t + 1):
            c.wait_send()

    @pl.when(t > 0)
    def _():
        for c in pass_q(t):
            c.wait_recv()

    for f in (0, 1):
        write(f, a, near).wait()
        write(f, 1 - a, far).wait()


def step(
    start_disp, start_vel, start_visc, init_state, inv_mass, damping_rate, visc_rate,
    fiber_stiff, fiber_family, pressure,
):
    hbm = pl.BlockSpec(memory_space=pltpu.HBM)
    out = jax.ShapeDtypeStruct((3, 4, 32, 256), F32)
    dma = pltpu.SemaphoreType.DMA
    outs = pl.pallas_call(
        kernel,
        out_shape=(out, out, jax.ShapeDtypeStruct((12, 32, 256), F32)),
        in_specs=[hbm] * 10,
        out_specs=(hbm, hbm, hbm),
        scratch_shapes=[
            pltpu.VMEM((STEPS + 1, 12, 2, ROWS, 128), F32),
            pltpu.VMEM((STEPS + 1, 12, 2, ROWS, 128), F32),
            pltpu.VMEM((12, 2, ROWS, 128), F32),
            pltpu.VMEM((6, 4, 2, ROWS, 128), F32),
            pltpu.VMEM((7, 2, ROWS, 128), F32),
            pltpu.VMEM((4, 2, ROWS, 128), F32),
            pltpu.VMEM((4, 2, ROWS, 128), F32),
            pltpu.VMEM((3, 8, 8), jnp.int32),
            pltpu.VMEM((6, 2, 32, 128), F32),
            pltpu.VMEM((3, 4, 32, 256), F32),
            pltpu.SMEM((1, 4), F32),
            pltpu.VMEM((2, 7, 4, ROWS, 128), F32),
            pltpu.VMEM((7, 4, ROWS, 128), F32),
            pltpu.VMEM((16, 8, 8, 128), F32),
            pltpu.VMEM((16, 8, 8, 128), F32),
            pltpu.VMEM((16, 4, 8, 128), F32),
            pltpu.VMEM((16, 6, 8, 128), F32),
            pltpu.VMEM((16, 6, 8, 128), F32),
            pltpu.VMEM((6, 4, 2, 32, 128), F32),
            pltpu.VMEM((6, 4, 32, 128), F32),
            dma((46,)), dma((2, 15)), dma((2, 15)), dma((3,)), dma((3,)), dma((2, 16)), dma((2, 16)),
            dma((2, 16)), dma((2, 16)), dma((3,)), dma((3,)), dma((10,)), dma((10,)), dma((2, 2)),
        ],
        compiler_params=pltpu.CompilerParams(
            collective_id=0, has_side_effects=True, vmem_limit_bytes=63 * 1024 * 1024
        ),
    )(
        start_disp.reshape(12, 32, 256),
        start_vel.reshape(12, 32, 256),
        start_visc.reshape(12, 32, 256),
        init_state.reshape(9, 4, 32, 256),
        inv_mass,
        damping_rate,
        visc_rate,
        fiber_stiff,
        fiber_family,
        pressure,
    )
    return tuple(x.reshape(1, 3, 4, 32, 256) for x in outs)


def solution(mesh):
    state = P("tm", None, None, "space", None)
    cell = P(None, "space", None)
    return jax.shard_map(
        step,
        mesh=mesh,
        in_specs=(
            state, state, state, P(None, None, None, "space", None),
            cell, cell, cell, cell, P("space", None), P("tm", None),
        ),
        out_specs=(state, state, state),
        check_vma=False,
    )
```

```python
import functools
import math

import jax
import jax.numpy as jnp
from jax import lax
from jax.experimental import pallas as pl
from jax.experimental.pallas import tpu as pltpu
from jax.sharding import PartitionSpec as P

MESH = pl.DeviceIdType.MESH
STEPS = 4
BLK_CIR = 32
AX = 0.22
RA = 0.12
CENTER = 2.0 * (AX + AX + RA)
SHARE = 0.6
F32 = jnp.float32
CHIPS = 16
PAUSE = 1

ROWS = 80
INNER = (1, 5)
OUTER = (6, 9)
EARLY = (0, 6)
LATE = (6, 2)


def expand(fam):
    col = lax.broadcasted_iota(jnp.int32, (8, 256), 1) // BLK_CIR
    row = lax.broadcasted_iota(jnp.int32, (8, 256), 0)
    return jnp.dot(
        fam.astype(F32), (col == row).astype(F32), preferred_element_type=F32
    )


def gmatrix(w, im, dp, fs):
    k = im * (CENTER + 2.0 * fs * w)
    hc = 2.0 * dp
    hk = 4.0 * k
    inv = 1.0 / (1.0 + hc + hk)
    return ((1.0 + hc - hk) * inv, 4.0 * inv, -hk * inv, (1.0 - hc - hk) * inv)


def rows(p, shift=0):
    return pl.ds(8 * p + shift, 8)


def kernel(
    sd, sv, sq, ini, im, dp, vr, fs, fam, prs,
    O, OQ,
    U, V, Q, M, T, SG, W, FM, IT, PR, Y, Z, S, R, GG, B, NR, E,
    ld, hs, hr, xs, xr, fsd, frc, bs, br, es, er, qs, qr,
):
    t = lax.axis_index("tm")
    sp = lax.axis_index("space")
    me = t // 2
    a = t % 2
    first = a == 0
    buddy = {"tm": me * 2 + (1 - a)}
    lanes = (pl.ds(0, 128), pl.ds(128, 128))

    def peer(k):
        i = k - 1
        j = i // 2
        hop = (j + 1) // 2
        along = jnp.where(lax.rem(j, 2) == 1, 4 - hop, 4 + hop)
        row = lax.rem(me // 8 + 1 - lax.rem(i, 2), 2)
        return row * 8 + lax.rem(lax.rem(me, 8) + along, 8)


    loads = []

    def load(src, dst):
        c = pltpu.make_async_copy(src, dst, ld.at[len(loads)])
        c.start()
        loads.append(c)

    states = ((sd, lambda *i: U.at[(0,) + i]), (sv, lambda *i: V.at[(0,) + i]), (sq, lambda *i: Q.at[i]))
    mats = tuple((m, lambda *i, k=k: M.at[(k,) + i]) for k, m in enumerate((im, dp, vr, fs)))
    fields = states + mats
    every = slice(None)
    for h in (0, 1):
        for src, dst in fields:
            load(src.at[:, :, lanes[h]], dst(every, h, pl.ds(8, 32)))
    load(fam, FM.at[0])
    load(prs, PR)
    rad_m, q_m = me // 4, me % 4
    initial = pltpu.make_async_copy(ini.at[pl.ds(6, 3)], OQ.reshape(3, 4, 32, 256), qr.at[0])

    @pl.when(t == 0)
    def _():
        initial.start()

    for h in (0, 1):
        load(ini.at[pl.ds(0, 6), rad_m, :, lanes[h]], IT.at[:, h])

    bar = pltpu.get_barrier_semaphore()

    def greet(k, _):
        d = lax.rem(me + k, CHIPS)
        pl.semaphore_signal(bar, inc=1, device_id={"tm": d * 2 + a}, device_id_type=MESH)
        return 0

    @pl.when(sp > 0)
    def _():
        pl.semaphore_signal(bar, inc=1, device_id={"space": sp - 1}, device_id_type=MESH)

    @pl.when(sp < 7)
    def _():
        pl.semaphore_signal(bar, inc=1, device_id={"space": sp + 1}, device_id_type=MESH)

    lax.fori_loop(1, CHIPS, greet, 0)
    pl.semaphore_signal(bar, inc=1, device_id=buddy, device_id_type=MESH)
    chain = jnp.logical_or(
        jnp.logical_and(a == 1, t < 31), jnp.logical_and(a == 0, t > 0)
    )
    mate = {"tm": jnp.where(a == 1, t + 1, t - 1)}

    @pl.when(chain)
    def _():
        pl.semaphore_signal(bar, inc=1, device_id=mate, device_id_type=MESH)

    for c in loads:
        c.wait()
    lane = lax.broadcasted_iota(jnp.int32, (8, 128), 1)

    def after(x):
        y = [pltpu.roll(k, 127, 1) for k in x]
        return [jnp.where(lane == 127, y[1 - h], y[h]) for h in (0, 1)]

    def before(x):
        y = [pltpu.roll(k, 1, 1) for k in x]
        return [jnp.where(lane == 0, y[1 - h], y[h]) for h in (0, 1)]

    upper = lax.broadcasted_iota(jnp.int32, (8, 256), 0) < 4

    def angles(p, one, two):
        f = jnp.where(
            upper, jnp.broadcast_to(one, (8, 256)), jnp.broadcast_to(two, (8, 256))
        )
        wide = f > 1.5
        co = jnp.where(wide, math.cos(0.9), math.cos(0.5)).astype(F32)
        si = jnp.where(wide, math.sin(0.9), math.sin(0.5)).astype(F32)
        odd = jnp.where(wide, f - 2.0, f) > 0.5
        si = jnp.where(odd, -si, si)
        co2, cs, si2 = [[x[:, :128], x[:, 128:]] for x in (co * co, co * si, si * si)]
        csc, si2c = before(cs), before(si2)
        for h in (0, 1):
            T[0, h, rows(p)] = co2[h]
            T[1, h, rows(p)] = cs[h]
            T[2, h, rows(p)] = si2[h]
            T[3, h, rows(p)] = co2[h] + cs[h]
            T[4, h, rows(p)] = cs[h] + si2[h]
            T[5, h, rows(p)] = csc[h]
            T[6, h, rows(p)] = si2c[h]

    def prepare(lo, hi):
        def rates(p, _):
            for h in (0, 1):
                for r in range(4):
                    d = jnp.exp(-M[2, r, h, rows(p)])
                    M[2, r, h, rows(p)] = d
                    M[4, r, h, rows(p)] = 1.0 - M[1, r, h, rows(p)]
                    M[5, r, h, rows(p)] = SHARE * (1.0 - d)
            return 0

        lax.fori_loop(lo, hi, rates, 0)

    def both(f):
        return [f(0), f(1)]

    def strains(s, p):
        co2, cs, si2 = [both(lambda h, k=k: T[k, h, rows(p)]) for k in range(3)]
        for r in range(4):
            u1 = both(lambda h: U[s, 4 + r, h, rows(p)])
            u2 = both(lambda h: U[s, 8 + r, h, rows(p)])
            c1, c2 = after(u1), after(u2)
            for h in (0, 1):
                d1 = U[s, 4 + r, h, rows(p, 1)] - u1[h]
                d2 = U[s, 8 + r, h, rows(p, 1)] - u2[h]
                e = co2[h] * d1 + si2[h] * (c2[h] - u2[h]) + cs[h] * (d2 + (c1[h] - u1[h]))
                w = jnp.exp(e * e)
                SG[r, h, rows(p)] = M[3, r, h, rows(p)] * w * e

                @pl.when(s == 0)
                def _(w=w, r=r, h=h):
                    W[r, h, rows(p)] = w

    def advance(s, p):
        for r in range(4):
            sg = both(lambda h: SG[r, h, rows(p)])
            sc = before(sg)
            f1, f2 = [], []
            for h in (0, 1):
                sb = SG[r, h, rows(p, -1)]
                f1.append(
                    T[3, h, rows(p)] * sg[h] - T[0, h, rows(p, -1)] * sb - T[5, h, rows(p)] * sc[h]
                )
                f2.append(
                    T[4, h, rows(p)] * sg[h] - T[1, h, rows(p, -1)] * sb - T[6, h, rows(p)] * sc[h]
                )
            force = (None, f1, f2)
            mass, d, keep, gain = [both(lambda h, k=k: M[k, r, h, rows(p)]) for k in (0, 2, 4, 5)]
            for c in range(3):
                i = c * 4 + r
                u = both(lambda h: U[s, i, h, rows(p)])
                ca, cb = after(u), before(u)
                for h in (0, 1):
                    near = (U[s, i, h, rows(p, 1)] + U[s, i, h, rows(p, -1)]) + (ca[h] + cb[h])
                    radial = U[s, i - 1, h, rows(p)] if r > 0 else U[s, i + 1, h, rows(p)]
                    if 0 < r < 3:
                        radial = radial + U[s, i + 1, h, rows(p)]
                    el = AX * near + RA * radial - CENTER * u[h]
                    q = Q[i, h, rows(p)]
                    total = el + q
                    if c:
                        total = total + force[c][h]
                    elif r == 0:
                        total = total + PR[0, s]
                    v = keep[h] * V[s, i, h, rows(p)] + mass[h] * total
                    V[s + 1, i, h, rows(p)] = v
                    U[s + 1, i, h, rows(p)] = u[h] + v
                    Q[i, h, rows(p)] = d[h] * q + gain[h] * el

    def steps(lo, hi, begin, end):
        def one(s, _):
            lax.fori_loop(lo, hi, lambda p, _: (strains(s, p), 0)[1], 0)
            lax.fori_loop(lo, hi, lambda p, _: (advance(s, p), 0)[1], 0)
            return 0

        lax.fori_loop(begin, end, one, 0)

    spread = expand(FM[0])
    for g in range(4):
        angles(1 + g, spread[2 * g : 2 * g + 1], spread[2 * g + 1 : 2 * g + 2])
    prepare(*INNER)
    steps(*INNER, 0, PAUSE)

    greeted = 16 + jnp.where(chain, 1, 0) + jnp.where(sp > 0, 1, 0) + jnp.where(sp < 7, 1, 0)
    pl.semaphore_wait(bar, greeted)

    def halo(side):
        cut, at, to = ((pl.ds(0, 4), pl.ds(56, 4), sp - 1), (pl.ds(28, 4), pl.ds(60, 4), sp + 1))[side]
        pairs = [(fam, FM.at[1 + side])]
        for src, dst in fields:
            for h in (0, 1):
                pairs.append((src.at[:, cut, lanes[h]], dst(every, h, at)))
        return [
            pltpu.make_async_remote_copy(
                src_ref=src, dst_ref=dst, send_sem=hs.at[side, i], recv_sem=hr.at[side, i],
                device_id={"space": to}, device_id_type=MESH,
            )
            for i, (src, dst) in enumerate(pairs)
        ]

    has_from = (sp < 7, sp > 0)
    has_to = (sp > 0, sp < 7)
    for side in (0, 1):

        @pl.when(has_to[side])
        def _(side=side):
            for c in halo(side):
                c.start()

    for edge, at in ((7, pl.ds(56, 4)), (0, pl.ds(60, 4))):

        @pl.when(sp == edge)
        def _(at=at):
            blank = jnp.zeros((4, 128), F32)
            for h in (0, 1):
                for i in range(12):
                    U[0, i, h, at] = blank
                    V[0, i, h, at] = blank
                    Q[i, h, at] = blank
                for k in range(4):
                    for r in range(4):
                        M[k, r, h, at] = blank

    inner_loads = len(loads)
    for h in (0, 1):
        for src, dst in fields:
            load(src.at[:, pl.ds(24, 8), lanes[h]], dst(every, h, pl.ds(48, 8)))
            load(src.at[:, pl.ds(0, 8), lanes[h]], dst(every, h, pl.ds(64, 8)))

    steps(*INNER, PAUSE, STEPS)

    def swap(p, slab):
        at = pl.ds(pl.multiple_of(8 * p, 8), 8)
        return pltpu.make_async_remote_copy(
            src_ref=Z.at[:, :, at], dst_ref=Y.at[slab, :, :, at],
            send_sem=xs.at[p], recv_sem=xr.at[p], device_id=buddy, device_id_type=MESH,
        )

    def maps(p):
        for r in range(4):

            def put(j, x, r=r):
                Y[a, j, r, rows(p)] = jnp.where(first, x[0], x[1])
                Z[j, r, rows(p)] = jnp.where(first, x[1], x[0])

            w = both(lambda h: W[r, h, rows(p)])
            g = both(
                lambda h: gmatrix(
                    w[h], M[0, r, h, rows(p)], M[1, r, h, rows(p)], M[3, r, h, rows(p)]
                )
            )
            put(6, w)
            for c in range(3):
                i = c * 4 + r
                cu, cv = [], []
                for h in (0, 1):
                    u0, v0 = U[0, i, h, rows(p)], V[0, i, h, rows(p)]
                    cu.append(U[STEPS, i, h, rows(p)] - (g[h][0] * u0 + g[h][1] * v0))
                    cv.append(V[STEPS, i, h, rows(p)] - (g[h][2] * u0 + g[h][3] * v0))
                put(c, cu)
                put(3 + c, cv)
        swap(p, a).start()

    def place(part, q):
        if part is EARLY:
            return 12 + 6 * q, 4 + 6 * q
        return jnp.where(q < 2, 64 + 2 * q, 48 + 2 * q), jnp.where(q < 2, 2 * q, 24 + 2 * q)

    def mix(part):
        return 0 if part is EARLY else 1

    def onward(part, d, slot):
        at = pl.ds(*part)
        return pltpu.make_async_remote_copy(
            src_ref=S.at[d, :, at], dst_ref=R.at[slot, :, at],
            send_sem=fsd.at[mix(part), d], recv_sem=frc.at[mix(part), slot],
            device_id={"tm": d * 2 + a}, device_id_type=MESH,
        )

    def compose(part):
        lo, n = part

        def tile(k, _):
            d = peer(k)
            r, q = d // 4, d % 4
            at = pl.ds(place(part, q)[0], n)
            w1 = Y[1, 6, r, at]
            g = gmatrix(w1, M[0, r, a, at], M[1, r, a, at], M[3, r, a, at])
            S[d, 6, lo : lo + n] = Y[0, 6, r, at]
            S[d, 7, lo : lo + n] = w1
            for c in range(3):
                cu, cv = Y[0, c, r, at], Y[0, 3 + c, r, at]
                S[d, c, lo : lo + n] = g[0] * cu + g[1] * cv + Y[1, c, r, at]
                S[d, 3 + c, lo : lo + n] = g[2] * cu + g[3] * cv + Y[1, 3 + c, r, at]

            @pl.when(d != me)
            def _():
                onward(part, d, me).start()

            return 0

        lax.fori_loop(1, CHIPS + 1, tile, 0)
        R[me, :, lo : lo + n] = S[me, :, lo : lo + n]

    lax.fori_loop(*INNER, lambda p, _: (maps(p), 0)[1], 0)
    for p in range(*INNER):
        swap(p, 1 - a).wait_recv()
    compose(EARLY)

    for side in (0, 1):

        @pl.when(has_from[side])
        def _(side=side):
            for c in halo(side):
                c.wait_recv()

    for c in loads[inner_loads:]:
        c.wait()
    after_row = expand(FM[1])[0:1]
    before_row = expand(FM[2])[7:8]
    angles(6, spread[6:7], spread[7:8])
    angles(7, after_row, before_row)
    angles(8, spread[0:1], spread[1:2])
    prepare(*OUTER)
    steps(*OUTER, 0, STEPS)
    lax.fori_loop(0, 2, lambda p, _: (maps(6 + 2 * p), 0)[1], 0)
    for p in (6, 8):
        swap(p, 1 - a).wait_recv()
    compose(LATE)

    def pass_q(to):
        made = []
        for src, dst, n in ((12, 4, 4), (16, 8, 16), (32, 24, 4), (52, 28, 4), (64, 0, 4)):
            for h in (0, 1):
                i = len(made)
                made.append(
                    pltpu.make_async_remote_copy(
                        src_ref=Q.at[:, h, pl.ds(src, n)], dst_ref=OQ.at[:, pl.ds(dst, n), lanes[h]],
                        send_sem=qs.at[i], recv_sem=qr.at[i], device_id={"tm": to}, device_id_type=MESH,
                    )
                )
        return made

    def back(part, c, slot):
        at = pl.ds(*part)
        return pltpu.make_async_remote_copy(
            src_ref=B.at[c, :, at], dst_ref=NR.at[slot, :, at],
            send_sem=bs.at[mix(part), c], recv_sem=br.at[mix(part), slot],
            device_id={"tm": c * 2 + a}, device_id_type=MESH,
        )

    def recur(part):
        lo, n = part
        at = slice(lo, lo + n)
        work, own = place(part, q_m)
        mine = [M[i, rad_m, a, pl.ds(work, n)] for i in (0, 1, 3)]

        def absorb(k, _):
            c = peer(k)

            @pl.when(c != me)
            def _():
                onward(part, c, c).wait_recv()

            ga = gmatrix(R[c, 6, at], *mine)
            gb = gmatrix(R[c, 7, at], *mine)
            GG[c, 0, at] = gb[0] * ga[0] + gb[1] * ga[2]
            GG[c, 1, at] = gb[0] * ga[1] + gb[1] * ga[3]
            GG[c, 2, at] = gb[2] * ga[0] + gb[3] * ga[2]
            GG[c, 3, at] = gb[2] * ga[1] + gb[3] * ga[3]
            return 0

        lax.fori_loop(1, CHIPS + 1, absorb, 0)

        def chip(c, now):
            for j in range(6):
                B[c, j, at] = now[j]

            g = [GG[c, j, at] for j in range(4)]
            us = [g[0] * now[j] + g[1] * now[3 + j] + R[c, j, at] for j in range(3)]
            vs = [g[2] * now[j] + g[3] * now[3 + j] + R[c, 3 + j, at] for j in range(3)]
            return tuple(us + vs)

        lax.fori_loop(0, CHIPS, chip, tuple(IT[j, a, pl.ds(own, n)] for j in range(6)))

        def reply(k, _):
            back(part, peer(k), me).start()
            return 0

        lax.fori_loop(1, CHIPS, reply, 0)
        NR[me, :, at] = B[me, :, at]

    def finish(part):
        lo, n = part
        at = slice(lo, lo + n)

        def tile(k, _):
            d = peer(k)

            @pl.when(d != me)
            def _():
                back(part, d, d).wait_recv()

            r, q = d // 4, d % 4
            work, own = place(part, q)
            work, own = pl.ds(work, n), pl.ds(own, n)
            g = gmatrix(Y[0, 6, r, work], M[0, r, a, work], M[1, r, a, work], M[3, r, a, work])
            for j in range(3):
                u, v = NR[d, j, at], NR[d, 3 + j, at]
                u1 = g[0] * u + g[1] * v + Y[0, j, r, work]
                v1 = g[2] * u + g[3] * v + Y[0, 3 + j, r, work]
                E[j, r, own] = jnp.where(first, u1, u)
                E[3 + j, r, own] = jnp.where(first, v1, v)
                O[j, r, a, own] = jnp.where(first, u, u1)
                O[3 + j, r, a, own] = jnp.where(first, v, v1)
            return 0

        lax.fori_loop(1, CHIPS + 1, tile, 0)

    spans = (pl.ds(8, 16), pl.ds(0, 8), pl.ds(24, 8))

    def deliver(i, h):
        return pltpu.make_async_remote_copy(
            src_ref=E.at[:, :, spans[i]], dst_ref=O.at[:, :, h, spans[i]],
            send_sem=es.at[i], recv_sem=er.at[i], device_id=buddy, device_id_type=MESH,
        )

    for p in (1, 2, 3, 4, 6, 8):
        swap(p, a).wait_send()
    for side in (0, 1):

        @pl.when(has_to[side])
        def _(side=side):
            for c in halo(side):
                c.wait_send()

    recur(EARLY)
    recur(LATE)

    @pl.when(t < 31)
    def _():
        for c in pass_q(t + 1):
            c.start()


    @pl.when(t < 31)
    def _():
        for c in pass_q(t + 1):
            c.wait_send()

    def settle(d, _):
        @pl.when(d != me)
        def _():
            for part in (EARLY, LATE):
                onward(part, d, me).wait_send()

        return 0

    lax.fori_loop(0, CHIPS, settle, 0)


    finish(EARLY)
    deliver(0, a).start()
    finish(LATE)
    for i in (1, 2):
        deliver(i, a).start()


    def sent(d, _):
        @pl.when(d != me)
        def _():
            for part in (EARLY, LATE):
                back(part, d, me).wait_send()

        return 0

    lax.fori_loop(0, CHIPS, sent, 0)
    for i in (0, 1, 2):
        deliver(i, 1 - a).wait_recv()
        deliver(i, a).wait_send()

    @pl.when(t == 0)
    def _():
        initial.wait()

    @pl.when(t > 0)
    def _():
        for c in pass_q(t):
            c.wait_recv()


def write_out(moved, visc, o_d, o_v, o_q, sem):
    copies = [pltpu.make_async_copy(visc, o_q, sem.at[4])]
    for f, out in enumerate((o_d, o_v)):
        for h in (0, 1):
            copies.append(
                pltpu.make_async_copy(
                    moved.at[pl.ds(3 * f, 3), :, h],
                    out.at[:, :, :, pl.ds(128 * h, 128)],
                    sem.at[2 * f + h],
                )
            )
    for c in copies:
        c.start()
    for c in copies:
        c.wait()


def step(
    start_disp, start_vel, start_visc, init_state, inv_mass, damping_rate, visc_rate,
    fiber_stiff, fiber_family, pressure,
):
    hbm = pl.BlockSpec(memory_space=pltpu.HBM)
    vmem = pl.BlockSpec(memory_space=pltpu.VMEM)
    dma = pltpu.SemaphoreType.DMA
    moved, visc = pl.pallas_call(
        kernel,
        out_shape=(pltpu.VMEM((6, 4, 2, 32, 128), F32), pltpu.VMEM((12, 32, 256), F32)),
        in_specs=[hbm] * 10,
        out_specs=(vmem, vmem),
        scratch_shapes=[
            pltpu.VMEM((STEPS + 1, 12, 2, ROWS, 128), F32),
            pltpu.VMEM((STEPS + 1, 12, 2, ROWS, 128), F32),
            pltpu.VMEM((12, 2, ROWS, 128), F32),
            pltpu.VMEM((6, 4, 2, ROWS, 128), F32),
            pltpu.VMEM((7, 2, ROWS, 128), F32),
            pltpu.VMEM((4, 2, ROWS, 128), F32),
            pltpu.VMEM((4, 2, ROWS, 128), F32),
            pltpu.VMEM((3, 8, 8), jnp.int32),
            pltpu.VMEM((6, 2, 32, 128), F32),
            pltpu.SMEM((1, 4), F32),
            pltpu.VMEM((2, 7, 4, ROWS, 128), F32),
            pltpu.VMEM((7, 4, ROWS, 128), F32),
            pltpu.VMEM((16, 8, 8, 128), F32),
            pltpu.VMEM((16, 8, 8, 128), F32),
            pltpu.VMEM((16, 4, 8, 128), F32),
            pltpu.VMEM((16, 6, 8, 128), F32),
            pltpu.VMEM((16, 6, 8, 128), F32),
            pltpu.VMEM((6, 4, 32, 128), F32),
            dma((46,)), dma((2, 15)), dma((2, 15)), dma((9,)), dma((9,)), dma((2, 16)), dma((2, 16)),
            dma((2, 16)), dma((2, 16)), dma((3,)), dma((3,)), dma((10,)), dma((10,)),
        ],
        compiler_params=pltpu.CompilerParams(
            collective_id=0, has_side_effects=True, vmem_limit_bytes=61000 * 1024
        ),
    )(
        start_disp.reshape(12, 32, 256),
        start_vel.reshape(12, 32, 256),
        start_visc.reshape(12, 32, 256),
        init_state.reshape(9, 4, 32, 256),
        inv_mass,
        damping_rate,
        visc_rate,
        fiber_stiff,
        fiber_family,
        pressure,
    )
    out = jax.ShapeDtypeStruct((3, 4, 32, 256), F32)
    outs = pl.pallas_call(
        write_out,
        out_shape=(out, out, jax.ShapeDtypeStruct((12, 32, 256), F32)),
        in_specs=[vmem, vmem],
        out_specs=(hbm, hbm, hbm),
        scratch_shapes=[dma((5,))],
        compiler_params=pltpu.CompilerParams(vmem_limit_bytes=8 * 1024 * 1024),
    )(moved, visc)
    return tuple(x.reshape(1, 3, 4, 32, 256) for x in outs)


def solution(mesh):
    state = P("tm", None, None, "space", None)
    cell = P(None, "space", None)
    return jax.shard_map(
        step,
        mesh=mesh,
        in_specs=(
            state, state, state, P(None, None, None, "space", None),
            cell, cell, cell, cell, P("space", None), P("tm", None),
        ),
        out_specs=(state, state, state),
        check_vma=False,
    )
```

```python
import functools
import math

import jax
import jax.numpy as jnp
from jax import lax
from jax.experimental import pallas as pl
from jax.experimental.pallas import tpu as pltpu
from jax.sharding import PartitionSpec as P

MESH = pl.DeviceIdType.MESH
STEPS = 4
BLK_CIR = 32
AX = 0.22
RA = 0.12
CENTER = 2.0 * (AX + AX + RA)
SHARE = 0.6
F32 = jnp.float32
CHIPS = 16
PAUSE = 1
WIDE = 3

ROWS = 80
INNER = (1, 5)
OUTER = (6, 9)
EARLY = (0, 6)
LATE = (6, 2)


def expand(fam):
    col = lax.broadcasted_iota(jnp.int32, (8, 256), 1) // BLK_CIR
    row = lax.broadcasted_iota(jnp.int32, (8, 256), 0)
    return jnp.dot(
        fam.astype(F32), (col == row).astype(F32), preferred_element_type=F32
    )


def gmatrix(w, im, dp, fs):
    k = im * (CENTER + 2.0 * fs * w)
    hc = 2.0 * dp
    hk = 4.0 * k
    inv = 1.0 / (1.0 + hc + hk)
    return ((1.0 + hc - hk) * inv, 4.0 * inv, -hk * inv, (1.0 - hc - hk) * inv)


def rows(p, shift=0):
    return pl.ds(8 * p + shift, 8)


def kernel(
    sd, sv, sq, ini, im, dp, vr, fs, fam, prs,
    O, OQ,
    U, V, Q, M, T, SG, W, FM, IT, PR, Y, Z, S, R, GG, B, NR, E,
    ld, hs, hr, xs, xr, fsd, frc, bs, br, es, er, qs, qr,
):
    t = lax.axis_index("tm")
    sp = lax.axis_index("space")
    me = t // 2
    a = t % 2
    first = a == 0
    buddy = {"tm": me * 2 + (1 - a)}
    lanes = (pl.ds(0, 128), pl.ds(128, 128))

    def peer(k):
        i = k - 1
        j = i // 2
        hop = (j + 1) // 2
        along = jnp.where(lax.rem(j, 2) == 1, 4 - hop, 4 + hop)
        row = lax.rem(me // 8 + 1 - lax.rem(i, 2), 2)
        return row * 8 + lax.rem(lax.rem(me, 8) + along, 8)


    loads = []

    def load(src, dst):
        c = pltpu.make_async_copy(src, dst, ld.at[len(loads)])
        c.start()
        loads.append(c)

    states = ((sd, lambda *i: U.at[(0,) + i]), (sv, lambda *i: V.at[(0,) + i]), (sq, lambda *i: Q.at[i]))
    mats = tuple((m, lambda *i, k=k: M.at[(k,) + i]) for k, m in enumerate((im, dp, vr, fs)))
    fields = states + mats
    every = slice(None)
    for h in (0, 1):
        for src, dst in fields:
            load(src.at[:, :, lanes[h]], dst(every, h, pl.ds(8, 32)))
    load(fam, FM.at[0])
    load(prs, PR)
    rad_m, q_m = me // 4, me % 4
    initial = pltpu.make_async_copy(ini.at[pl.ds(6, 3)], OQ.reshape(3, 4, 32, 256), qr.at[0])

    @pl.when(t == 0)
    def _():
        initial.start()

    for h in (0, 1):
        load(ini.at[pl.ds(0, 6), rad_m, :, lanes[h]], IT.at[:, h])

    bar = pltpu.get_barrier_semaphore()

    def greet(k, _):
        d = lax.rem(me + k, CHIPS)
        pl.semaphore_signal(bar, inc=1, device_id={"tm": d * 2 + a}, device_id_type=MESH)
        return 0

    @pl.when(sp > 0)
    def _():
        pl.semaphore_signal(bar, inc=1, device_id={"space": sp - 1}, device_id_type=MESH)

    @pl.when(sp < 7)
    def _():
        pl.semaphore_signal(bar, inc=1, device_id={"space": sp + 1}, device_id_type=MESH)

    lax.fori_loop(1, CHIPS, greet, 0)
    pl.semaphore_signal(bar, inc=1, device_id=buddy, device_id_type=MESH)
    chain = jnp.logical_or(
        jnp.logical_and(a == 1, t < 31), jnp.logical_and(a == 0, t > 0)
    )
    mate = {"tm": jnp.where(a == 1, t + 1, t - 1)}

    @pl.when(chain)
    def _():
        pl.semaphore_signal(bar, inc=1, device_id=mate, device_id_type=MESH)

    for c in loads:
        c.wait()
    lane = lax.broadcasted_iota(jnp.int32, (8, 128), 1)

    def after(x):
        y = [pltpu.roll(k, 127, 1) for k in x]
        return [jnp.where(lane == 127, y[1 - h], y[h]) for h in (0, 1)]

    def before(x):
        y = [pltpu.roll(k, 1, 1) for k in x]
        return [jnp.where(lane == 0, y[1 - h], y[h]) for h in (0, 1)]

    upper = lax.broadcasted_iota(jnp.int32, (8, 256), 0) < 4

    def angles(p, one, two):
        f = jnp.where(
            upper, jnp.broadcast_to(one, (8, 256)), jnp.broadcast_to(two, (8, 256))
        )
        wide = f > 1.5
        co = jnp.where(wide, math.cos(0.9), math.cos(0.5)).astype(F32)
        si = jnp.where(wide, math.sin(0.9), math.sin(0.5)).astype(F32)
        odd = jnp.where(wide, f - 2.0, f) > 0.5
        si = jnp.where(odd, -si, si)
        co2, cs, si2 = [[x[:, :128], x[:, 128:]] for x in (co * co, co * si, si * si)]
        csc, si2c = before(cs), before(si2)
        for h in (0, 1):
            T[0, h, rows(p)] = co2[h]
            T[1, h, rows(p)] = cs[h]
            T[2, h, rows(p)] = si2[h]
            T[3, h, rows(p)] = co2[h] + cs[h]
            T[4, h, rows(p)] = cs[h] + si2[h]
            T[5, h, rows(p)] = csc[h]
            T[6, h, rows(p)] = si2c[h]

    def prepare(lo, hi):
        def rates(p, _):
            for h in (0, 1):
                for r in range(4):
                    d = jnp.exp(-M[2, r, h, rows(p)])
                    M[2, r, h, rows(p)] = d
                    M[4, r, h, rows(p)] = 1.0 - M[1, r, h, rows(p)]
                    M[5, r, h, rows(p)] = SHARE * (1.0 - d)
            return 0

        lax.fori_loop(lo, hi, rates, 0)

    def both(f):
        return [f(0), f(1)]

    def strains(s, p):
        co2, cs, si2 = [both(lambda h, k=k: T[k, h, rows(p)]) for k in range(3)]
        for r in range(4):
            u1 = both(lambda h: U[s, 4 + r, h, rows(p)])
            u2 = both(lambda h: U[s, 8 + r, h, rows(p)])
            c1, c2 = after(u1), after(u2)
            for h in (0, 1):
                d1 = U[s, 4 + r, h, rows(p, 1)] - u1[h]
                d2 = U[s, 8 + r, h, rows(p, 1)] - u2[h]
                e = co2[h] * d1 + si2[h] * (c2[h] - u2[h]) + cs[h] * (d2 + (c1[h] - u1[h]))
                w = jnp.exp(e * e)
                SG[r, h, rows(p)] = M[3, r, h, rows(p)] * w * e

                @pl.when(s == 0)
                def _(w=w, r=r, h=h):
                    W[r, h, rows(p)] = w

    def advance(s, p):
        for r in range(4):
            sg = both(lambda h: SG[r, h, rows(p)])
            sc = before(sg)
            f1, f2 = [], []
            for h in (0, 1):
                sb = SG[r, h, rows(p, -1)]
                f1.append(
                    T[3, h, rows(p)] * sg[h] - T[0, h, rows(p, -1)] * sb - T[5, h, rows(p)] * sc[h]
                )
                f2.append(
                    T[4, h, rows(p)] * sg[h] - T[1, h, rows(p, -1)] * sb - T[6, h, rows(p)] * sc[h]
                )
            force = (None, f1, f2)
            mass, d, keep, gain = [both(lambda h, k=k: M[k, r, h, rows(p)]) for k in (0, 2, 4, 5)]
            for c in range(3):
                i = c * 4 + r
                u = both(lambda h: U[s, i, h, rows(p)])
                ca, cb = after(u), before(u)
                for h in (0, 1):
                    near = (U[s, i, h, rows(p, 1)] + U[s, i, h, rows(p, -1)]) + (ca[h] + cb[h])
                    radial = U[s, i - 1, h, rows(p)] if r > 0 else U[s, i + 1, h, rows(p)]
                    if 0 < r < 3:
                        radial = radial + U[s, i + 1, h, rows(p)]
                    el = AX * near + RA * radial - CENTER * u[h]
                    q = Q[i, h, rows(p)]
                    total = el + q
                    if c:
                        total = total + force[c][h]
                    elif r == 0:
                        total = total + PR[0, s]
                    v = keep[h] * V[s, i, h, rows(p)] + mass[h] * total
                    V[s + 1, i, h, rows(p)] = v
                    U[s + 1, i, h, rows(p)] = u[h] + v
                    Q[i, h, rows(p)] = d[h] * q + gain[h] * el

    def steps(lo, hi, begin, end):
        def one(s, _):
            lax.fori_loop(lo, hi, lambda p, _: (strains(s, p), 0)[1], 0, unroll=2)
            lax.fori_loop(lo, hi, lambda p, _: (advance(s, p), 0)[1], 0, unroll=2)
            return 0

        lax.fori_loop(begin, end, one, 0)

    spread = expand(FM[0])
    for g in range(4):
        angles(1 + g, spread[2 * g : 2 * g + 1], spread[2 * g + 1 : 2 * g + 2])
    prepare(*INNER)
    steps(*INNER, 0, PAUSE)

    greeted = 16 + jnp.where(chain, 1, 0) + jnp.where(sp > 0, 1, 0) + jnp.where(sp < 7, 1, 0)
    pl.semaphore_wait(bar, greeted)

    def halo(side):
        to = (sp - 1, sp + 1)[side]
        pairs = [(fam, FM.at[1 + side])]
        for i, (src, dst) in enumerate(fields):
            n = 4 if i in (0, 6) else 3
            cut, at = ((0, 56), (32 - n, 64 - n))[side]
            for h in (0, 1):
                pairs.append((src.at[:, pl.ds(cut, n), lanes[h]], dst(every, h, pl.ds(at, n))))
        return [
            pltpu.make_async_remote_copy(
                src_ref=src, dst_ref=dst, send_sem=hs.at[side, i], recv_sem=hr.at[side, i],
                device_id={"space": to}, device_id_type=MESH,
            )
            for i, (src, dst) in enumerate(pairs)
        ]

    has_from = (sp < 7, sp > 0)
    has_to = (sp > 0, sp < 7)
    for side in (0, 1):

        @pl.when(has_to[side])
        def _(side=side):
            for c in halo(side):
                c.start()

    steps(*INNER, PAUSE, STEPS)

    def swap(p, slab):
        at = pl.ds(pl.multiple_of(8 * p, 8), 8)
        return pltpu.make_async_remote_copy(
            src_ref=Z.at[:, :, at], dst_ref=Y.at[slab, :, :, at],
            send_sem=xs.at[p], recv_sem=xr.at[p], device_id=buddy, device_id_type=MESH,
        )

    def maps(p):
        for r in range(4):

            def put(j, x, r=r):
                Y[a, j, r, rows(p)] = jnp.where(first, x[0], x[1])
                Z[j, r, rows(p)] = jnp.where(first, x[1], x[0])

            w = both(lambda h: W[r, h, rows(p)])
            g = both(
                lambda h: gmatrix(
                    w[h], M[0, r, h, rows(p)], M[1, r, h, rows(p)], M[3, r, h, rows(p)]
                )
            )
            put(6, w)
            for c in range(3):
                i = c * 4 + r
                cu, cv = [], []
                for h in (0, 1):
                    u0, v0 = U[0, i, h, rows(p)], V[0, i, h, rows(p)]
                    cu.append(U[STEPS, i, h, rows(p)] - (g[h][0] * u0 + g[h][1] * v0))
                    cv.append(V[STEPS, i, h, rows(p)] - (g[h][2] * u0 + g[h][3] * v0))
                put(c, cu)
                put(3 + c, cv)
        swap(p, a).start()

    def place(part, q):
        if part is EARLY:
            return 12 + 6 * q, 4 + 6 * q
        return jnp.where(q < 2, 64 + 2 * q, 48 + 2 * q), jnp.where(q < 2, 2 * q, 24 + 2 * q)

    def mix(part):
        return 0 if part is EARLY else 1

    def onward(part, d, slot):
        at = pl.ds(*part)
        return pltpu.make_async_remote_copy(
            src_ref=S.at[d, :, at], dst_ref=R.at[slot, :, at],
            send_sem=fsd.at[mix(part), d], recv_sem=frc.at[mix(part), slot],
            device_id={"tm": d * 2 + a}, device_id_type=MESH,
        )

    def compose(part):
        lo, n = part

        def tile(d):
            r, q = d // 4, d % 4
            at = pl.ds(place(part, q)[0], n)
            w1 = Y[1, 6, r, at]
            g = gmatrix(w1, M[0, r, a, at], M[1, r, a, at], M[3, r, a, at])
            S[d, 6, lo : lo + n] = Y[0, 6, r, at]
            S[d, 7, lo : lo + n] = w1
            for c in range(3):
                cu, cv = Y[0, c, r, at], Y[0, 3 + c, r, at]
                S[d, c, lo : lo + n] = g[0] * cu + g[1] * cv + Y[1, c, r, at]
                S[d, 3 + c, lo : lo + n] = g[2] * cu + g[3] * cv + Y[1, 3 + c, r, at]

        def batch(i, _):
            peers = [peer(WIDE * i + j + 1) for j in range(WIDE)]
            for d in peers:
                tile(d)
            for d in peers:
                onward(part, d, me).start()
            return 0

        lax.fori_loop(0, 15 // WIDE, batch, 0)
        tile(me)
        R[me, :, lo : lo + n] = S[me, :, lo : lo + n]

    lax.fori_loop(*INNER, lambda p, _: (maps(p), 0)[1], 0)
    inner_loads = len(loads)
    for h in (0, 1):
        for src, dst in fields:
            load(src.at[:, pl.ds(24, 8), lanes[h]], dst(every, h, pl.ds(48, 8)))
            load(src.at[:, pl.ds(0, 8), lanes[h]], dst(every, h, pl.ds(64, 8)))

    for edge, at in ((7, pl.ds(56, 4)), (0, pl.ds(60, 4))):

        @pl.when(sp == edge)
        def _(at=at):
            blank = jnp.zeros((4, 128), F32)
            for h in (0, 1):
                for i in range(12):
                    U[0, i, h, at] = blank
                    V[0, i, h, at] = blank
                    Q[i, h, at] = blank
                for k in range(4):
                    for r in range(4):
                        M[k, r, h, at] = blank

    for p in range(*INNER):
        swap(p, 1 - a).wait_recv()
    compose(EARLY)

    for side in (0, 1):

        @pl.when(has_from[side])
        def _(side=side):
            for c in halo(side):
                c.wait_recv()

    for c in loads[inner_loads:]:
        c.wait()
    after_row = expand(FM[1])[0:1]
    before_row = expand(FM[2])[7:8]
    angles(6, spread[6:7], spread[7:8])
    angles(7, after_row, before_row)
    angles(8, spread[0:1], spread[1:2])
    prepare(*OUTER)
    steps(*OUTER, 0, STEPS)
    lax.fori_loop(0, 2, lambda p, _: (maps(6 + 2 * p), 0)[1], 0)
    for p in (6, 8):
        swap(p, 1 - a).wait_recv()
    compose(LATE)

    def pass_q(to):
        made = []
        for src, dst, n in ((12, 4, 4), (16, 8, 16), (32, 24, 4), (52, 28, 4), (64, 0, 4)):
            for h in (0, 1):
                i = len(made)
                made.append(
                    pltpu.make_async_remote_copy(
                        src_ref=Q.at[:, h, pl.ds(src, n)], dst_ref=OQ.at[:, pl.ds(dst, n), lanes[h]],
                        send_sem=qs.at[i], recv_sem=qr.at[i], device_id={"tm": to}, device_id_type=MESH,
                    )
                )
        return made

    def back(part, c, slot):
        at = pl.ds(*part)
        return pltpu.make_async_remote_copy(
            src_ref=B.at[c, :, at], dst_ref=NR.at[slot, :, at],
            send_sem=bs.at[mix(part), c], recv_sem=br.at[mix(part), slot],
            device_id={"tm": c * 2 + a}, device_id_type=MESH,
        )

    def recur(part):
        lo, n = part
        at = slice(lo, lo + n)
        work, own = place(part, q_m)
        mine = [M[i, rad_m, a, pl.ds(work, n)] for i in (0, 1, 3)]

        def absorb(c):
            ga = gmatrix(R[c, 6, at], *mine)
            gb = gmatrix(R[c, 7, at], *mine)
            GG[c, 0, at] = gb[0] * ga[0] + gb[1] * ga[2]
            GG[c, 1, at] = gb[0] * ga[1] + gb[1] * ga[3]
            GG[c, 2, at] = gb[2] * ga[0] + gb[3] * ga[2]
            GG[c, 3, at] = gb[2] * ga[1] + gb[3] * ga[3]

        def batch(i, _):
            peers = [peer(WIDE * i + j + 1) for j in range(WIDE)]
            for c in peers:
                onward(part, c, c).wait_recv()
            for c in peers:
                absorb(c)
            return 0

        absorb(me)
        lax.fori_loop(0, 15 // WIDE, batch, 0)

        def chip(c, now):
            for j in range(6):
                B[c, j, at] = now[j]

            g = [GG[c, j, at] for j in range(4)]
            us = [g[0] * now[j] + g[1] * now[3 + j] + R[c, j, at] for j in range(3)]
            vs = [g[2] * now[j] + g[3] * now[3 + j] + R[c, 3 + j, at] for j in range(3)]
            return tuple(us + vs)

        lax.fori_loop(
            0, CHIPS, chip, tuple(IT[j, a, pl.ds(own, n)] for j in range(6)), unroll=4
        )

        def reply(k, _):
            back(part, peer(k), me).start()
            return 0

        lax.fori_loop(1, CHIPS, reply, 0)
        NR[me, :, at] = B[me, :, at]

    def finish(part):
        lo, n = part
        at = slice(lo, lo + n)

        def tile(d):
            r, q = d // 4, d % 4
            work, own = place(part, q)
            work, own = pl.ds(work, n), pl.ds(own, n)
            g = gmatrix(Y[0, 6, r, work], M[0, r, a, work], M[1, r, a, work], M[3, r, a, work])
            for j in range(3):
                u, v = NR[d, j, at], NR[d, 3 + j, at]
                u1 = g[0] * u + g[1] * v + Y[0, j, r, work]
                v1 = g[2] * u + g[3] * v + Y[0, 3 + j, r, work]
                E[j, r, own] = jnp.where(first, u1, u)
                E[3 + j, r, own] = jnp.where(first, v1, v)
                O[j, r, a, own] = jnp.where(first, u, u1)
                O[3 + j, r, a, own] = jnp.where(first, v, v1)

        def batch(i, _):
            peers = [peer(WIDE * i + j + 1) for j in range(WIDE)]
            for d in peers:
                back(part, d, d).wait_recv()
            for d in peers:
                tile(d)
            return 0

        tile(me)
        lax.fori_loop(0, 15 // WIDE, batch, 0)

    spans = (pl.ds(8, 16), pl.ds(0, 8), pl.ds(24, 8))

    def deliver(i, h):
        return pltpu.make_async_remote_copy(
            src_ref=E.at[:, :, spans[i]], dst_ref=O.at[:, :, h, spans[i]],
            send_sem=es.at[i], recv_sem=er.at[i], device_id=buddy, device_id_type=MESH,
        )

    for p in (1, 2, 3, 4, 6, 8):
        swap(p, a).wait_send()
    for side in (0, 1):

        @pl.when(has_to[side])
        def _(side=side):
            for c in halo(side):
                c.wait_send()

    recur(EARLY)
    recur(LATE)

    @pl.when(t < 31)
    def _():
        for c in pass_q(t + 1):
            c.start()


    @pl.when(t < 31)
    def _():
        for c in pass_q(t + 1):
            c.wait_send()

    def settle(d, _):
        @pl.when(d != me)
        def _():
            for part in (EARLY, LATE):
                onward(part, d, me).wait_send()

        return 0

    lax.fori_loop(0, CHIPS, settle, 0)


    finish(EARLY)
    deliver(0, a).start()
    finish(LATE)
    for i in (1, 2):
        deliver(i, a).start()


    def sent(d, _):
        @pl.when(d != me)
        def _():
            for part in (EARLY, LATE):
                back(part, d, me).wait_send()

        return 0

    lax.fori_loop(0, CHIPS, sent, 0)
    for i in (0, 1, 2):
        deliver(i, 1 - a).wait_recv()
        deliver(i, a).wait_send()

    @pl.when(t == 0)
    def _():
        initial.wait()

    @pl.when(t > 0)
    def _():
        for c in pass_q(t):
            c.wait_recv()


def write_out(moved, visc, o_d, o_v, o_q, sem):
    copies = [pltpu.make_async_copy(visc, o_q, sem.at[4])]
    for f, out in enumerate((o_d, o_v)):
        for h in (0, 1):
            copies.append(
                pltpu.make_async_copy(
                    moved.at[pl.ds(3 * f, 3), :, h],
                    out.at[:, :, :, pl.ds(128 * h, 128)],
                    sem.at[2 * f + h],
                )
            )
    for c in copies:
        c.start()
    for c in copies:
        c.wait()


def step(
    start_disp, start_vel, start_visc, init_state, inv_mass, damping_rate, visc_rate,
    fiber_stiff, fiber_family, pressure,
):
    hbm = pl.BlockSpec(memory_space=pltpu.HBM)
    vmem = pl.BlockSpec(memory_space=pltpu.VMEM)
    dma = pltpu.SemaphoreType.DMA
    moved, visc = pl.pallas_call(
        kernel,
        out_shape=(pltpu.VMEM((6, 4, 2, 32, 128), F32), pltpu.VMEM((12, 32, 256), F32)),
        in_specs=[hbm] * 10,
        out_specs=(vmem, vmem),
        scratch_shapes=[
            pltpu.VMEM((STEPS + 1, 12, 2, ROWS, 128), F32),
            pltpu.VMEM((STEPS + 1, 12, 2, ROWS, 128), F32),
            pltpu.VMEM((12, 2, ROWS, 128), F32),
            pltpu.VMEM((6, 4, 2, ROWS, 128), F32),
            pltpu.VMEM((7, 2, ROWS, 128), F32),
            pltpu.VMEM((4, 2, ROWS, 128), F32),
            pltpu.VMEM((4, 2, ROWS, 128), F32),
            pltpu.VMEM((3, 8, 8), jnp.int32),
            pltpu.VMEM((6, 2, 32, 128), F32),
            pltpu.SMEM((1, 4), F32),
            pltpu.VMEM((2, 7, 4, ROWS, 128), F32),
            pltpu.VMEM((7, 4, ROWS, 128), F32),
            pltpu.VMEM((16, 8, 8, 128), F32),
            pltpu.VMEM((16, 8, 8, 128), F32),
            pltpu.VMEM((16, 4, 8, 128), F32),
            pltpu.VMEM((16, 6, 8, 128), F32),
            pltpu.VMEM((16, 6, 8, 128), F32),
            pltpu.VMEM((6, 4, 32, 128), F32),
            dma((46,)), dma((2, 15)), dma((2, 15)), dma((9,)), dma((9,)), dma((2, 16)), dma((2, 16)),
            dma((2, 16)), dma((2, 16)), dma((3,)), dma((3,)), dma((10,)), dma((10,)),
        ],
        compiler_params=pltpu.CompilerParams(
            collective_id=0, has_side_effects=True, vmem_limit_bytes=61000 * 1024
        ),
    )(
        start_disp.reshape(12, 32, 256),
        start_vel.reshape(12, 32, 256),
        start_visc.reshape(12, 32, 256),
        init_state.reshape(9, 4, 32, 256),
        inv_mass,
        damping_rate,
        visc_rate,
        fiber_stiff,
        fiber_family,
        pressure,
    )
    out = jax.ShapeDtypeStruct((3, 4, 32, 256), F32)
    outs = pl.pallas_call(
        write_out,
        out_shape=(out, out, jax.ShapeDtypeStruct((12, 32, 256), F32)),
        in_specs=[vmem, vmem],
        out_specs=(hbm, hbm, hbm),
        scratch_shapes=[dma((5,))],
        compiler_params=pltpu.CompilerParams(vmem_limit_bytes=8 * 1024 * 1024),
    )(moved, visc)
    return tuple(x.reshape(1, 3, 4, 32, 256) for x in outs)


def solution(mesh):
    state = P("tm", None, None, "space", None)
    cell = P(None, "space", None)
    return jax.shard_map(
        step,
        mesh=mesh,
        in_specs=(
            state, state, state, P(None, None, None, "space", None),
            cell, cell, cell, cell, P("space", None), P("tm", None),
        ),
        out_specs=(state, state, state),
        check_vma=False,
    )
```
